32 devices in a mesh: land: 8 (over y, x, core), sea: 4 (over z).
Axes of the slice: x: 2, y: 2, z: 4, core: 2. Of those that a mesh axis runs over, the one named last changes fastest.
Arguments:
- adj_depth: float32 [4096, 2048], P('land', 'sea'), may hold values from -6 to 6
- conductance: float32 [4096, 2048], P('land', 'sea'), may hold values from 0.02 to 0.24
- wet: int32 [4, 4096, 2048], P(None, 'land', 'sea'), may hold values 0 or 1
- coast_cell: int32 [262144], P(('land', 'sea')), may hold values from 0 to 262143
- coast_dest: int32 [262144, 1], P(('land', 'sea')), may hold values from 0 to 31; in each aligned block of 8192 rows (0 to 8191, 8192 to 16383, ...) at most 512 rows name the same one
- coast_node: int32 [262144], P(('land', 'sea')), may hold values from 0 to 16383
- coast_weight: float32 [262144], P(('land', 'sea')), may hold values from 0.2 to 2
- adj_ocean: float32 [4096, 128], P(('land', 'sea')), may hold values from -6 to 6
- ocean_blocks: bfloat16 [4096, 2, 128, 128], P(('land', 'sea')), may hold values from -0.375 to 0.375
- ocean_target: int32 [4096, 2], P(('land', 'sea')), may hold values from 0 to 511
Outputs:
- land_out: float32 [4096, 2048], P('land', 'sea')
- ocean_out: float32 [4096, 128], P(('land', 'sea'))
The draws below stay inside these ranges and needn't reach their ends.
Inputs may be any that keep to these rules, and one draw needn't show every extreme that they name: `coast_dest`: in each device's 8192 rows no partition is named by more than 512 entries, and one is named by exactly 512. `ocean_target`: blocks are numbered within the group of the 4 devices that share a land index.
All inputs are finite; a program needn't handle non-finite values. No bound on the sum of `wet` on one device may be relied on, other than what follows from the above.
Results may differ from the reference program's by a relative error of at most 0.0036.
Values sent between devices are 32-bit elements; how exact they have to be, the bound alone decides.
A program may use at most 128 MiB of HBM per device.

```python
import math
import jax
import jax.numpy as jnp
import numpy as np
from jax import lax

RX = 512
RY = 512
NB = 128
BS = 128
KB = 2
CL = 8192
STEPS = 4
MOST = 512
NXR = 4096
NYR = 2048
OBLK = 512
NBLK = 4096
NCOAST = 262144
N_SEA = 4
DEVICES = 32


def with_ends(result, stream_key, low, high):
    longest = result.shape.index(max(result.shape))
    spots = []
    for shift in (0, 1):
        where = [jax.random.randint(jax.random.fold_in(stream_key, axis), (), 0, length) for axis, length in enumerate(result.shape)]
        where[longest] = (where[longest] + shift) % result.shape[longest]
        spots.append(tuple(where))
    return result.at[spots[0]].set(low).at[spots[1]].set(high)


def levels(own_key, dims, pieces, low, top_value):
    factor_of, own = 1.0, jax.random.fold_in(own_key, 6)
    for position, shards_of in pieces:
        steps = jnp.exp(jax.random.uniform(jax.random.fold_in(own, position), (shards_of,), jnp.float32, low / len(pieces), top_value / len(pieces)))
        factor_of = factor_of * jnp.repeat(steps, dims[position] // shards_of).reshape([-1 if axis == position else 1 for axis in range(len(dims))])
    return factor_of


def shared_out(rng, own, number, rows, amount, top, limit, lean):
    ranking = jax.random.permutation(rng, amount)
    crowded, common = portions_of(amount, rows * top, limit, lean, True), portions_of(amount, rows * top, limit, lean, False)
    places = jnp.arange(amount)

    def named(tallies, offset_by):
        used = int((tallies > 0).sum())
        fixed = max(1, used // 4)
        shifted = fixed + (places - fixed + offset_by * (used - fixed)) % max(1, amount - fixed)
        return jnp.zeros((amount,), jnp.int32).at[ranking[jnp.where(places < fixed, places, shifted)]].set(jnp.asarray(tallies, jnp.int32))

    tallies = jnp.where(number % 4 == 0, named(crowded, number // 4), named(common, number - number // 4 - 1))
    mixed = jax.random.permutation(jax.random.fold_in(own, 3), amount)
    donor, taker = mixed[0:amount // 2 * 2:2], mixed[1:amount // 2 * 2:2]
    slack = jnp.minimum(tallies[donor] - 1, limit - tallies[taker]) // 2
    slack = jnp.where((donor == ranking[0]) | (taker == ranking[0]) | (tallies[taker] == 0), 0, jnp.maximum(slack, 0))
    shifted = jax.random.randint(jax.random.fold_in(own, 4), (amount // 2,), 0, 1 << 20) % (slack + 1)
    tallies = tallies.at[donor].add(-shifted).at[taker].add(shifted)
    items = jnp.searchsorted(jnp.cumsum(tallies), jnp.arange(rows * top), side="right").astype(jnp.int32)
    table = items.reshape(top, rows).T
    table = table[jax.random.permutation(jax.random.fold_in(own, 1), rows)]
    offset_by = jax.random.randint(jax.random.fold_in(own, 2), (rows, 1), 0, top)
    return jnp.take_along_axis(table, (jnp.arange(top)[None, :] + offset_by) % top, axis=1)


def portions_of(amount, total, limit, skew, full):
    loads = [(1 << 20) // math.isqrt(rank ** skew) + 1 for rank in range(1, amount + 1)]
    largest = limit if full else min(limit, max(-(-total // amount), total * loads[0] // sum(loads)))
    least = 1 if total - largest >= amount - 1 else 0
    given, rest = [largest] + [least] * (amount - 1), total - largest - least * (amount - 1)
    while rest > 0:
        movable = [i for i in range(1, amount) if given[i] < largest] or [i for i in range(1, amount) if given[i] < limit]
        mass, left = sum([loads[i] for i in movable]), rest
        for i in movable:
            more = min(limit - given[i], max(1, left * loads[i] // mass), rest)
            given[i] = given[i] + more
            rest = rest - more
    return np.array(given)


def centred(stream_key, shape, scale, limit, pieces=(), dtype=jnp.bfloat16):
    entries = jax.random.normal(stream_key, shape, jnp.float32) * scale
    if len(pieces) > 0:
        entries = levels(stream_key, shape, pieces, -0.22, 0.18) * entries
    return jnp.clip(entries, min=-limit, max=limit).astype(dtype)


def setup_inputs(seed: int = 0) -> dict:
    key_list = jax.random.split(jax.random.key(seed), 11)
    adj_depth = centred(key_list[0], (NXR, NYR), 1.0, 6.0, ((0, 8), (1, 4)), jnp.float32)
    conductance = jnp.clip(0.02 + 0.22 * jax.random.uniform(key_list[1], (NXR, NYR), jnp.float32) ** levels(key_list[1], (NXR, NYR), ((0, 8), (1, 4)), -0.2, 0.2), 0.02, 0.24)
    wet = with_ends((jax.random.randint(key_list[2], (STEPS, NXR, NYR), 0, 4) < 3).astype(jnp.int32), jax.random.fold_in(key_list[2], 1), 0, 1)
    coast_cell = with_ends(jax.random.randint(key_list[3], (NCOAST,), 0, RX * RY), jax.random.fold_in(key_list[3], 1), 0, (RX * RY) - 1).astype(jnp.int32)
    coast_dest_keys = jax.random.split(jax.random.fold_in(key_list[4], 1), NCOAST // CL)
    coast_dest_turns = jax.random.permutation(jax.random.fold_in(key_list[4], 3), NCOAST // CL)
    coast_dest = jax.vmap(lambda own, number: shared_out(jax.random.fold_in(key_list[4], 2), own, number, CL, DEVICES, 1, MOST, 2))(coast_dest_keys, coast_dest_turns).reshape((NCOAST, 1))
    coast_node = with_ends(jax.random.randint(key_list[5], (NCOAST,), 0, NB * BS), jax.random.fold_in(key_list[5], 1), 0, (NB * BS) - 1).astype(jnp.int32)
    coast_weight = jnp.clip(jnp.exp(math.log(2.0) - 2.3025851 * jax.random.uniform(key_list[6], (NCOAST,), jnp.float32) ** levels(key_list[6], (NCOAST,), ((0, 32),), -0.2, 0.2)), 0.2, 2.0)
    adj_ocean = centred(key_list[7], (NBLK, BS), 1.0, 6.0, ((0, 32),), jnp.float32)
    ocean_blocks = centred(key_list[8], (NBLK, KB, BS, BS), (BS * KB) ** -0.5, 0.375, ((0, 32),))
    ocean_target = with_ends(jax.random.randint(key_list[9], (NBLK, KB), 0, OBLK), jax.random.fold_in(key_list[9], 1), 0, OBLK - 1).astype(jnp.int32)
    return dict(adj_depth=adj_depth, conductance=conductance, wet=wet, coast_cell=coast_cell, coast_dest=coast_dest, coast_node=coast_node, coast_weight=coast_weight, adj_ocean=adj_ocean, ocean_blocks=ocean_blocks, ocean_target=ocean_target)


def laplace_zero(spread):
    padded = jnp.pad(spread, 1)
    beside_all = padded[2:, 1:-1] + padded[:-2, 1:-1] + padded[1:-1, 2:] + padded[1:-1, :-2]
    return beside_all - 4.0 * spread


def block_terms(pair):
    weights, vector = pair
    return jnp.einsum("bkij,bi->bkj", weights.astype(jnp.float32), vector.astype(jnp.float32))


def reference(adj_depth, conductance, wet, coast_cell, coast_dest, coast_node, coast_weight, adj_ocean, ocean_blocks, ocean_target):
    source_dev = (jnp.arange(DEVICES * CL) // CL).astype(jnp.int32)
    cell_row = (source_dev // N_SEA) * RX + coast_cell // RY
    cell_col = (source_dev % N_SEA) * RY + coast_cell % RY
    node_global = coast_dest[:, 0] * (NB * BS) + coast_node
    block_dev = (jnp.arange(DEVICES * NB) // NB).astype(jnp.int32)
    target_global = ((block_dev // N_SEA) * (NB * N_SEA))[:, None] + ocean_target
    target_global = target_global.reshape(-1)
    land_adj = adj_depth
    ocean_adj = adj_ocean
    grouped = ocean_blocks.reshape(DEVICES, NB, KB, BS, BS)
    for timestep in range(STEPS):
        wet_now = wet[timestep].astype(jnp.float32)
        flux = coast_weight * wet_now[cell_row, cell_col] * land_adj[cell_row, cell_col]
        coupled = jnp.zeros((NB * DEVICES * BS,), jnp.float32).at[node_global].add(flux)
        coupled = coupled.reshape(NB * DEVICES, BS)
        ocean_low = ocean_adj.astype(jnp.bfloat16)
        terms = lax.map(block_terms, (grouped, ocean_low.reshape(DEVICES, NB, BS)))
        partial_sum = jnp.zeros((NB * DEVICES, BS), jnp.float32).at[target_global].add(terms.reshape(-1, BS))
        ocean_adj = 0.5 * ocean_adj + partial_sum + coupled
        spread = conductance * wet_now * land_adj
        land_adj = land_adj + laplace_zero(spread)
    return land_adj, ocean_adj
```

```python
import functools

import jax
import jax.numpy as jnp
from jax import lax
from jax.experimental import pallas as pl
from jax.experimental.pallas import tpu as pltpu
from jax.sharding import PartitionSpec as P

STEPS = 4
LANES = 128
SUB = 8
HALO = STEPS


MESH = pl.DeviceIdType.MESH


def beside_of(axis):
    count, me = lax.axis_size(axis), lax.axis_index(axis)
    return lax.rem(me + count - 1, count), lax.rem(me + 1, count)


def land_kernel(depth, cond, wet, out, masked, ext, out_edge, in_edge, sends, recvs):
    rows, cols = depth.shape
    total = 2 + STEPS
    used = total * HALO
    height, width = ext.shape[1], ext.shape[2]
    mid_r, mid_c = pl.ds(SUB, rows), pl.ds(LANES, cols)
    west, east = beside_of("sea")
    north, south = beside_of("land")

    barrier = pltpu.get_barrier_semaphore()
    for to in ({"sea": west}, {"sea": east}, {"land": north}, {"land": south}):
        pl.semaphore_signal(barrier, inc=1, device_id=to, device_id_type=MESH)

    ext[0, mid_r, mid_c] = depth[...]
    ext[1, mid_r, mid_c] = cond[...]
    for t in range(STEPS):
        ext[2 + t, mid_r, mid_c] = wet[t].astype(jnp.float32)

    lane = lax.broadcasted_iota(jnp.int32, (rows, LANES), 1)

    def gathered(start, first):
        edge = jnp.zeros((rows, LANES), jnp.float32)
        for i in range(total):
            tile = ext[i, mid_r, pl.ds(start, LANES)]
            shift = (i * HALO - first) % LANES
            tile = pltpu.roll(tile, shift, 1) if shift else tile
            edge = jnp.where(lane // HALO == i, tile, edge)
        return edge.T[:used]

    out_edge[0] = gathered(LANES, 0)
    out_edge[1] = gathered(cols, LANES - HALO)
    for side in range(2):
        in_edge[side, used:, :] = jnp.zeros((LANES - used, rows), jnp.float32)
    pl.semaphore_wait(barrier, 4)

    copies = [
        pltpu.make_async_remote_copy(
            src_ref=out_edge.at[side],
            dst_ref=in_edge.at[side, pl.ds(0, used)],
            send_sem=sends.at[side],
            recv_sem=recvs.at[side],
            device_id={"sea": to},
            device_id_type=MESH,
        )
        for side, to in ((0, west), (1, east))
    ]
    for copy in copies:
        copy.start()
    for copy in copies:
        copy.wait()

    def spread_out(side, start, first, present):
        edge = in_edge[side].T
        for i in range(total):
            shift = (first - i * HALO) % LANES
            tile = pltpu.roll(edge, shift, 1) if shift else edge
            keep = (lane >= first) & (lane < first + HALO) & present
            ext[i, mid_r, pl.ds(start, LANES)] = jnp.where(keep, tile, 0.0)

    sea, seas = lax.axis_index("sea"), lax.axis_size("sea")
    land, lands = lax.axis_index("land"), lax.axis_size("land")
    spread_out(1, 0, LANES - HALO, sea > 0)
    spread_out(0, LANES + cols, 0, sea < seas - 1)

    copies = [
        pltpu.make_async_remote_copy(
            src_ref=ext.at[:, pl.ds(source, SUB), :],
            dst_ref=ext.at[:, pl.ds(target, SUB), :],
            send_sem=sends.at[slot],
            recv_sem=recvs.at[slot],
            device_id={"land": to},
            device_id_type=MESH,
        )
        for slot, source, target, to in (
            (2, SUB, SUB + rows, north),
            (3, rows, 0, south),
        )
    ]
    for copy in copies:
        copy.start()
    for copy in copies:
        copy.wait()
    for start, present in ((0, land > 0), (SUB + rows, land < lands - 1)):
        strip = ext[1, pl.ds(start, SUB), :]
        ext[1, pl.ds(start, SUB), :] = strip * jnp.where(present, 1.0, 0.0)

    for t in range(STEPS):
        wet_land = ext[2 + t] * ext[0]
        masked[t] = wet_land[SUB : SUB + rows, LANES : LANES + cols].astype(jnp.bfloat16)
        spread = ext[1] * wet_land
        beside = (
            pltpu.roll(spread, 1, 0)
            + pltpu.roll(spread, height - 1, 0)
            + pltpu.roll(spread, 1, 1)
            + pltpu.roll(spread, width - 1, 1)
        )
        ext[0] = ext[0] + (beside - 4.0 * spread)
    out[...] = ext[0, mid_r, mid_c]


def land_steps(depth, cond, wet):
    rows, cols = depth.shape
    total = 2 + STEPS
    vmem = pl.BlockSpec(memory_space=pltpu.VMEM)
    return pl.pallas_call(
        land_kernel,
        out_shape=(
            jax.ShapeDtypeStruct((rows, cols), jnp.float32),
            jax.ShapeDtypeStruct((STEPS, rows, cols), jnp.bfloat16),
        ),
        in_specs=[vmem] * 3,
        out_specs=(vmem, vmem),
        scratch_shapes=[
            pltpu.VMEM((total, rows + 2 * SUB, cols + 2 * LANES), jnp.float32),
            pltpu.VMEM((2, total * HALO, rows), jnp.float32),
            pltpu.VMEM((2, LANES, rows), jnp.float32),
            pltpu.SemaphoreType.DMA((4,)),
            pltpu.SemaphoreType.DMA((4,)),
        ],
        compiler_params=pltpu.CompilerParams(
            vmem_limit_bytes=40 << 20, collective_id=0, has_side_effects=True
        ),
        name="land_steps",
    )(depth, cond, wet)


def iota(shape, axis):
    return lax.broadcasted_iota(jnp.int32, shape, axis)


def halves(value):
    high = value.astype(jnp.bfloat16).astype(jnp.float32)
    return high, value - high


def across(a, b):
    return lax.dot_general(
        a, b, (((1,), (1,)), ((), ())), preferred_element_type=jnp.float32
    )


def placed(row, lane, values, rows):
    count = row.shape[1]
    row_hot = jnp.where(iota((rows, count), 0) == row, 1.0, 0.0).astype(jnp.bfloat16)
    lane_is = iota((LANES, count), 0) == lane
    spreads = [jnp.where(lane_is, v, 0.0).astype(jnp.bfloat16) for v in values]
    return across(row_hot, jnp.concatenate(spreads, axis=0))


def send_kernel(capacity, piece, cell, dest, node, weight, masked, out, acc, carry):
    step = pl.program_id(0)
    devices = carry.shape[0]
    cols = masked.shape[2]
    count = cell.shape[2]

    @pl.when(step == 0)
    def _():
        acc[...] = jnp.zeros_like(acc)
        carry[...] = jnp.zeros_like(carry)

    dest_now = dest[0]
    matches = jnp.where(iota((devices, count), 0) == dest_now, 1.0, 0.0)
    triangle = jnp.where(
        iota((piece, piece), 0) <= iota((piece, piece), 1), 1.0, 0.0
    ).astype(jnp.bfloat16)
    base = carry[:, 0:1]
    ranks = []
    for p in range(count // piece):
        own = matches[:, p * piece : (p + 1) * piece]
        running = jnp.dot(
            own.astype(jnp.bfloat16), triangle, preferred_element_type=jnp.float32
        )
        ranks.append(jnp.sum(own * (running + base), axis=0, keepdims=True))
        base = base + jnp.sum(own, axis=1, keepdims=True)
    carry[...] = jnp.broadcast_to(base, carry.shape)
    rank = jnp.concatenate(ranks, axis=1).astype(jnp.int32) - 1
    slot = dest_now * capacity + rank

    place = cell[0]
    cell_row, cell_col = place // cols, place % cols
    col_hot = jnp.where(iota((cols, count), 0) == cell_col, 1.0, 0.0).astype(jnp.bfloat16)
    row_is = iota((masked.shape[1], count), 0) == cell_row
    values = []
    for t in range(STEPS):
        lines = jnp.dot(masked[t], col_hot, preferred_element_type=jnp.float32)
        found = jnp.sum(jnp.where(row_is, lines, 0.0), axis=0, keepdims=True)
        values.extend(halves(weight[0] * found))
    node_now = node[0]
    values.append((node_now // LANES).astype(jnp.float32))
    values.append((node_now % LANES).astype(jnp.float32))
    acc[...] += placed(slot // LANES, slot % LANES, values, acc.shape[0])

    @pl.when(step == pl.num_programs(0) - 1)
    def _():
        def block(i):
            return acc[:, i * LANES : (i + 1) * LANES]

        for t in range(STEPS):
            out[t] = block(2 * t) + block(2 * t + 1)
        out[STEPS] = block(2 * STEPS) * float(LANES) + block(2 * STEPS + 1)


def packed(masked, cell, dest, node, weight, devices):
    entries = cell.shape[0]
    count = 1024
    steps = entries // count
    capacity = 2 * entries // devices
    rows = devices * capacity // LANES
    line = pl.BlockSpec((1, 1, count), lambda i: (i, 0, 0))
    shape = (steps, 1, count)
    return pl.pallas_call(
        functools.partial(send_kernel, capacity, 256),
        grid=(steps,),
        in_specs=[line] * 4 + [pl.BlockSpec(masked.shape, lambda i: (0, 0, 0))],
        out_specs=pl.BlockSpec((STEPS + 1, rows, LANES), lambda i: (0, 0, 0)),
        out_shape=jax.ShapeDtypeStruct((STEPS + 1, rows, LANES), jnp.float32),
        scratch_shapes=[
            pltpu.VMEM((rows, (2 * STEPS + 2) * LANES), jnp.float32),
            pltpu.VMEM((devices, LANES), jnp.float32),
        ],
        compiler_params=pltpu.CompilerParams(vmem_limit_bytes=48 << 20),
        name="coast_pack",
    )(cell.reshape(shape), dest.reshape(shape), node.reshape(shape), weight.reshape(shape), masked)


def partner_of(index):
    seas = lax.axis_size("sea")
    return {"land": index // seas, "sea": lax.rem(index, seas)}


def ocean_kernel(
    packs, operator, target, adj, out,
    held, got, terms, summed, parts, hot, row_hot, lane_hot, cur,
    load_sem, pack_sends, pack_recvs, sends, recvs,
):
    group, sea = lax.axis_size("sea"), lax.axis_index("sea")
    devices = group * lax.axis_size("land")
    me = lax.axis_index("land") * group + sea
    blocks, width = adj.shape
    kb = operator.shape[1]
    planes, capr = got.shape[0], got.shape[2]
    chunks = row_hot.shape[0]
    lines = row_hot.shape[2] // LANES

    load = pltpu.make_async_copy(operator, held, load_sem)
    load.start()
    barrier = pltpu.get_barrier_semaphore()

    def greet(d, _):
        to = partner_of(lax.rem(me + d, devices))
        pl.semaphore_signal(barrier, inc=1, device_id=to, device_id_type=MESH)
        return 0

    lax.fori_loop(1, devices, greet, 0)
    cur[...] = adj[...]
    for s in range(group):
        at = iota((blocks, kb * blocks), 0) + s * blocks
        hot[s * blocks : (s + 1) * blocks, :] = jnp.where(at == target[...], 1.0, 0.0).astype(
            jnp.bfloat16
        )
    pl.semaphore_wait(barrier, devices - 1)

    for p in [planes - 1] + list(range(planes - 1)):
        def send(d, _, p=p):
            index = lax.rem(me + d, devices)
            pltpu.make_async_remote_copy(
                src_ref=packs.at[p, index],
                dst_ref=got.at[p, me],
                send_sem=pack_sends.at[p],
                recv_sem=pack_recvs.at[p],
                device_id=partner_of(index),
                device_id_type=MESH,
            ).start()
            return 0

        lax.fori_loop(1, devices, send, 0)
        got[p, me] = packs[p, me]

    def arrived(p):
        pltpu.make_async_remote_copy(
            src_ref=packs.at[p, pl.ds(0, devices - 1)],
            dst_ref=got.at[p, pl.ds(0, devices - 1)],
            send_sem=pack_sends.at[p],
            recv_sem=pack_recvs.at[p],
            device_id=partner_of(lax.rem(me + 1, devices)),
            device_id_type=MESH,
        ).wait()

    def line(p, i):
        rows = []
        for k in range(lines):
            rows.append(got[p, i * (lines // capr) + k // capr, pl.ds(k % capr, 1), :])
        return jnp.concatenate(rows, axis=1)

    others = [lax.rem(sea + d, group) for d in range(1, group)]

    def exchange(t):
        return [
            pltpu.make_async_remote_copy(
                src_ref=summed.at[t, to],
                dst_ref=parts.at[t, i],
                send_sem=sends.at[t, i],
                recv_sem=recvs.at[t, i],
                device_id={"sea": to},
                device_id_type=MESH,
            )
            for i, to in enumerate(others)
        ]

    def step_terms(t):
        tall = 16
        for g in range(blocks // tall):
            own = cur[g * tall : (g + 1) * tall, :]
            sub = iota((tall, width), 0)
            wide = jnp.concatenate(
                [jnp.where(sub == j, own, 0.0).astype(jnp.bfloat16) for j in range(tall)], axis=1
            )
            for k in range(kb):
                block = held[g * tall : (g + 1) * tall, k].reshape(tall * width, width)
                terms[k * blocks + g * tall : k * blocks + (g + 1) * tall, :] = jnp.dot(
                    wide, block, preferred_element_type=jnp.float32
                )
        high, low = halves(terms[...])
        both = jnp.concatenate([high.astype(jnp.bfloat16), low.astype(jnp.bfloat16)], axis=1)
        total = jnp.dot(hot[...], both, preferred_element_type=jnp.float32)
        for s in range(group):
            rows = total[s * blocks : (s + 1) * blocks]
            summed[t, s] = rows[:, :width] + rows[:, width:]
        copies = exchange(t)
        for copy in copies:
            copy.start()
        return copies

    load.wait()
    copies = step_terms(0)

    arrived(planes - 1)

    def index_hots(i, _):
        node = line(planes - 1, i).astype(jnp.int32)
        at = iota((LANES, lines * LANES), 0)
        row_hot[i] = jnp.where(at == node // LANES, 1.0, 0.0).astype(jnp.bfloat16)
        lane_hot[i] = jnp.where(at == node % LANES, 1.0, 0.0).astype(jnp.bfloat16)
        return 0

    lax.fori_loop(0, chunks, index_hots, 0)

    for t in range(STEPS):
        arrived(t)

        def couple(i, acc, t=t):
            value = line(t, i).astype(jnp.bfloat16)
            return acc + across(row_hot[i], lane_hot[i] * value)

        coupled = lax.fori_loop(0, chunks, couple, jnp.zeros((blocks, width), jnp.float32))
        result = 0.5 * cur[...] + coupled + summed[t, sea]
        for copy in copies:
            copy.wait()
        for i in range(group - 1):
            result = result + parts[t, i]
        if t < STEPS - 1:
            cur[...] = result
            copies = step_terms(t + 1)
        else:
            out[...] = result


def ocean_steps(packs, operator, target, adj):
    group, devices = lax.axis_size("sea"), lax.axis_size(("land", "sea"))
    blocks, width = adj.shape
    kb = operator.shape[1]
    planes, _, capr, _ = packs.shape
    count = 1024
    chunks = devices * capr * LANES // count
    vmem = pl.BlockSpec(memory_space=pltpu.VMEM)
    return pl.pallas_call(
        ocean_kernel,
        out_shape=jax.ShapeDtypeStruct((blocks, width), jnp.float32),
        in_specs=[vmem, pl.BlockSpec(memory_space=pl.ANY), vmem, vmem],
        out_specs=vmem,
        scratch_shapes=[
            pltpu.VMEM(operator.shape, jnp.bfloat16),
            pltpu.VMEM(packs.shape, jnp.float32),
            pltpu.VMEM((kb * blocks, width), jnp.float32),
            pltpu.VMEM((STEPS, group, blocks, width), jnp.float32),
            pltpu.VMEM((STEPS, group - 1, blocks, width), jnp.float32),
            pltpu.VMEM((group * blocks, kb * blocks), jnp.bfloat16),
            pltpu.VMEM((chunks, blocks, count), jnp.bfloat16),
            pltpu.VMEM((chunks, LANES, count), jnp.bfloat16),
            pltpu.VMEM((blocks, width), jnp.float32),
            pltpu.SemaphoreType.DMA,
            pltpu.SemaphoreType.DMA((planes,)),
            pltpu.SemaphoreType.DMA((planes,)),
            pltpu.SemaphoreType.DMA((STEPS, group - 1)),
            pltpu.SemaphoreType.DMA((STEPS, group - 1)),
        ],
        compiler_params=pltpu.CompilerParams(
            vmem_limit_bytes=48 << 20, collective_id=1, has_side_effects=True
        ),
        name="ocean_steps",
    )(packs, operator, target, adj)


def local(
    adj_depth,
    conductance,
    wet,
    coast_cell,
    coast_dest,
    coast_node,
    coast_weight,
    adj_ocean,
    ocean_blocks,
    ocean_target,
):
    devices = lax.axis_size(("land", "sea"))
    land_out, masked = land_steps(adj_depth, conductance, wet)
    packs = packed(masked, coast_cell, coast_dest, coast_node, coast_weight, devices)
    packs = packs.reshape(STEPS + 1, devices, -1, LANES)
    target_row = ocean_target.T.reshape(1, -1)
    ocean_adj = ocean_steps(packs, ocean_blocks, target_row, adj_ocean)
    return (land_out, ocean_adj)


def solution(mesh):
    in_specs = (
        P("land", "sea"),
        P("land", "sea"),
        P(None, "land", "sea"),
        P(("land", "sea")),
        P(("land", "sea"), None),
        P(("land", "sea")),
        P(("land", "sea")),
        P(("land", "sea"), None),
        P(("land", "sea"), None, None, None),
        P(("land", "sea"), None),
    )
    out_specs = (P("land", "sea"), P(("land", "sea"), None))
    return jax.shard_map(local, mesh=mesh, in_specs=in_specs, out_specs=out_specs, check_vma=False)
```

```python
import jax
import jax.numpy as jnp
from jax import lax
from jax.experimental import pallas as pl
from jax.experimental.pallas import tpu as pltpu
from jax.sharding import PartitionSpec as P

STEPS = 4
LANES = 128
SUB = 8
COUNT = 1024
PIECE = 256
MESH = pl.DeviceIdType.MESH
f32, bf16 = jnp.float32, jnp.bfloat16


def iota(shape, axis):
    return lax.broadcasted_iota(jnp.int32, shape, axis)


def halves(value):
    high = value.astype(bf16)
    return high, (value - high.astype(f32)).astype(bf16)


def across(a, b):
    return lax.dot_general(a, b, (((1,), (1,)), ((), ())), preferred_element_type=f32)


def one_hot(index, size):
    return jnp.where(iota((size, index.shape[1]), 0) == index, 1.0, 0.0).astype(bf16)


def beside_of(axis):
    count, me = lax.axis_size(axis), lax.axis_index(axis)
    return lax.rem(me + count - 1, count), lax.rem(me + 1, count)


def partner_of(index):
    seas = lax.axis_size("sea")
    return {"land": index // seas, "sea": lax.rem(index, seas)}


def step_kernel(
    depth_in, cond_in, wet_in, cell_in, dest_in, node_in, weight_in, operator_in,
    target, adj, land_out, ocean_out,
    land, cond, wet, cell, dest, node, weight, held,
    ext, masked, col_hot, cell_row, slot_row, slot_lane, packs, got, node_row, node_lane,
    out_edge, in_edge, cur, terms, hot, summed, parts,
    loads, edge_sends, edge_recvs, pack_sends, pack_recvs, sends, recvs,
):
    group, sea = lax.axis_size("sea"), lax.axis_index("sea")
    lands, row_of = lax.axis_size("land"), lax.axis_index("land")
    devices, me = group * lands, row_of * group + sea
    rows, cols = land.shape
    blocks, width = adj.shape
    kb = held.shape[1]
    planes, capr = got.shape[0], got.shape[2]
    capacity = capr * LANES
    chunks, got_chunks = cell.shape[0], node_row.shape[0]
    lines = COUNT // LANES
    west, east = beside_of("sea")
    north, south = beside_of("land")

    pairs = [
        (cell_in, cell), (dest_in, dest), (node_in, node), (weight_in, weight),
        (depth_in, land), (wet_in.at[0], wet.at[0]), (cond_in, cond), (operator_in, held),
    ] + [(wet_in.at[t], wet.at[t]) for t in range(1, STEPS)]
    load = [pltpu.make_async_copy(a, b, loads.at[i]) for i, (a, b) in enumerate(pairs)]
    for copy in load:
        copy.start()

    barrier = pltpu.get_barrier_semaphore()

    def greet(d, _):
        to = partner_of(lax.rem(me + d, devices))
        pl.semaphore_signal(barrier, inc=1, device_id=to, device_id_type=MESH)
        return 0

    lax.fori_loop(1, devices, greet, 0)

    cur[...] = adj[...]
    for s in range(group):
        hot[s * blocks : (s + 1) * blocks, :] = one_hot(target[...] - s * blocks, blocks)
    others = [lax.rem(sea + d, group) for d in range(1, group)]

    def step_terms(t):
        tall = 16
        sub = iota((tall, width), 0)
        for g in range(blocks // tall):
            own = cur[g * tall : (g + 1) * tall, :]
            wide = jnp.concatenate(
                [jnp.where(sub == j, own, 0.0).astype(bf16) for j in range(tall)], axis=1
            )
            for k in range(kb):
                block = held[g * tall : (g + 1) * tall, k].reshape(tall * width, width)
                terms[k * blocks + g * tall : k * blocks + (g + 1) * tall, :] = jnp.dot(
                    wide, block, preferred_element_type=f32
                )
        both = jnp.concatenate(halves(terms[...]), axis=1)
        total = jnp.dot(hot[...], both, preferred_element_type=f32)
        for s in range(group):
            part = total[s * blocks : (s + 1) * blocks]
            summed[t, s] = part[:, :width] + part[:, width:]
        copies = [
            pltpu.make_async_remote_copy(
                src_ref=summed.at[t, to],
                dst_ref=parts.at[t, i],
                send_sem=sends.at[t, i],
                recv_sem=recvs.at[t, i],
                device_id={"sea": to},
                device_id_type=MESH,
            )
            for i, to in enumerate(others)
        ]
        for copy in copies:
            copy.start()
        return copies

    def send_plane(p, slots):
        for d in range(packs.shape[1]):
            packs[p, d] = slots[d * capr : (d + 1) * capr]

        def send(d, _):
            index = lax.rem(me + d, devices)
            pltpu.make_async_remote_copy(
                src_ref=packs.at[p, index],
                dst_ref=got.at[p, me],
                send_sem=pack_sends.at[p],
                recv_sem=pack_recvs.at[p],
                device_id=partner_of(index),
                device_id_type=MESH,
            ).start()
            return 0

        lax.fori_loop(1, devices, send, 0)
        got[p, me] = packs[p, me]

    def arrived(p):
        pltpu.make_async_remote_copy(
            src_ref=packs.at[p, pl.ds(0, devices - 1)],
            dst_ref=got.at[p, pl.ds(0, devices - 1)],
            send_sem=pack_sends.at[p],
            recv_sem=pack_recvs.at[p],
            device_id=partner_of(lax.rem(me + 1, devices)),
            device_id_type=MESH,
        ).wait()

    def line(p, i):
        return jnp.concatenate(
            [got[p, i * lines // capr + k // capr, pl.ds(k % capr, 1), :] for k in range(lines)],
            axis=1,
        )

    def spread_of(t):
        masked_step = wet[t].astype(f32) * land[...]
        masked[...] = masked_step.astype(bf16)
        ext[SUB : SUB + rows, LANES : LANES + cols] = cond[...] * masked_step
        first = ext[SUB : SUB + rows, LANES : 2 * LANES]
        last = ext[SUB : SUB + rows, cols : cols + LANES]
        sides = jnp.where(iota((rows, LANES), 1) < LANES // 2, first, last).T
        out_edge[t, 0] = ext[SUB : SUB + 1, LANES : LANES + cols]
        out_edge[t, 1] = ext[SUB + rows - 1 : SUB + rows, LANES : LANES + cols]
        out_edge[t, 2] = sides[0:1]
        out_edge[t, 3] = sides[LANES - 1 :]
        copies = [
            pltpu.make_async_remote_copy(
                src_ref=out_edge.at[t, i],
                dst_ref=in_edge.at[t, i ^ 1],
                send_sem=edge_sends.at[t, i],
                recv_sem=edge_recvs.at[t, i ^ 1],
                device_id=to,
                device_id_type=MESH,
            )
            for i, to in enumerate(
                ({"land": north}, {"land": south}, {"sea": west}, {"sea": east})
            )
        ]
        for copy in copies:
            copy.start()
        return copies

    def land_step(t, copies):
        for copy in copies:
            copy.wait()
        has = [jnp.where(c, 1.0, 0.0) for c in (row_of > 0, row_of < lands - 1, sea > 0, sea < group - 1)]
        ext[SUB - 1 : SUB, LANES : LANES + cols] = in_edge[t, 0] * has[0]
        ext[SUB + rows : SUB + rows + 1, LANES : LANES + cols] = in_edge[t, 1] * has[1]
        sub = iota((LANES, rows), 0)
        sides = jnp.where(
            sub == LANES - 1,
            in_edge[t, 2] * has[2],
            jnp.where(sub == 0, in_edge[t, 3] * has[3], 0.0),
        ).T
        ext[SUB : SUB + rows, 0:LANES] = sides
        ext[SUB : SUB + rows, LANES + cols :] = sides
        tall = min(rows, 128)
        for r in range(0, rows, tall):
            a = SUB + r
            spread = ext[a : a + tall, LANES : LANES + cols]
            beside = (
                ext[a - 1 : a - 1 + tall, LANES : LANES + cols]
                + ext[a + 1 : a + 1 + tall, LANES : LANES + cols]
                + ext[a : a + tall, LANES - 1 : LANES - 1 + cols]
                + ext[a : a + tall, LANES + 1 : LANES + 1 + cols]
            )
            land[r : r + tall] = land[r : r + tall] + (beside - 4.0 * spread)

    for i in range(3):
        load[i].wait()
    triangle = jnp.where(iota((PIECE, PIECE), 0) <= iota((PIECE, PIECE), 1), 1.0, 0.0).astype(bf16)

    def index_chunk(i, carry):
        base, nodes = carry
        dest_now, place, node_now = dest[i], cell[i], node[i]
        matches = jnp.where(iota((devices, COUNT), 0) == dest_now, 1.0, 0.0)
        ranks = []
        for p in range(0, COUNT, PIECE):
            own = matches[:, p : p + PIECE]
            running = jnp.dot(own.astype(bf16), triangle, preferred_element_type=f32)
            ranks.append(jnp.sum(own * (running + base), axis=0, keepdims=True))
            base = base + jnp.sum(own, axis=1, keepdims=True)
        rank = jnp.concatenate(ranks, axis=1).astype(jnp.int32) - 1
        slot = dest_now * capacity + rank
        at_row, at_lane = one_hot(slot // LANES, slot_row.shape[1]), one_hot(slot % LANES, LANES)
        slot_row[i], slot_lane[i] = at_row, at_lane
        col_hot[i] = one_hot(place % cols, cols)
        cell_row[i] = place // cols
        digits = [at_lane * d.astype(f32).astype(bf16) for d in (node_now // LANES, node_now % LANES)]
        return base, nodes + across(at_row, jnp.concatenate(digits, axis=0))

    _, nodes = lax.fori_loop(
        0,
        chunks,
        index_chunk,
        (jnp.zeros((devices, 1), f32), jnp.zeros((slot_row.shape[1], 2 * LANES), f32)),
    )
    pl.semaphore_wait(barrier, devices - 1)
    send_plane(planes - 1, nodes[:, :LANES] * float(LANES) + nodes[:, LANES:])

    def flux_plane(t):
        def chunk(i, slots):
            found = jnp.dot(masked[...], col_hot[i], preferred_element_type=f32)
            here = iota((rows, COUNT), 0) == cell_row[i]
            found = jnp.sum(jnp.where(here, found, 0.0), axis=0, keepdims=True)
            flux = (weight[i] * found).astype(bf16)
            return slots + across(slot_row[i], slot_lane[i] * flux)

        slots = lax.fori_loop(
            0, chunks, chunk, jnp.zeros((slot_row.shape[1], LANES), f32), unroll=True
        )
        send_plane(t, slots)

    def node_hots():
        arrived(planes - 1)

        def chunk(i, _):
            place = line(planes - 1, i).astype(jnp.int32)
            node_row[i] = one_hot(place // LANES, blocks)
            node_lane[i] = one_hot(place % LANES, LANES)
            return 0

        lax.fori_loop(0, got_chunks, chunk, 0)

    def ocean_step(t, copies):
        arrived(t)

        def chunk(i, acc):
            return acc + across(node_row[i], node_lane[i] * line(t, i).astype(bf16))

        coupled = lax.fori_loop(0, got_chunks, chunk, jnp.zeros((blocks, width), f32), unroll=True)
        result = 0.5 * cur[...] + coupled + summed[t, sea]
        for copy in copies:
            copy.wait()
        for i in range(group - 1):
            result = result + parts[t, i]
        return result

    for i in (4, 5, 6):
        load[i].wait()
    edges = spread_of(0)
    load[7].wait()
    shares = step_terms(0)
    load[3].wait()
    for copy in load[8:]:
        copy.wait()
    flux_plane(0)
    for t in range(1, STEPS):
        land_step(t - 1, edges)
        edges = spread_of(t)
        if t == 1:
            node_hots()
        flux_plane(t)
        cur[...] = ocean_step(t - 1, shares)
        shares = step_terms(t)
    land_step(STEPS - 1, edges)
    store = pltpu.make_async_copy(land, land_out, loads.at[0])
    store.start()
    ocean_out[...] = ocean_step(STEPS - 1, shares)
    store.wait()


def local(
    adj_depth,
    conductance,
    wet,
    coast_cell,
    coast_dest,
    coast_node,
    coast_weight,
    adj_ocean,
    ocean_blocks,
    ocean_target,
):
    group, devices = lax.axis_size("sea"), lax.axis_size(("land", "sea"))
    rows, cols = adj_depth.shape
    blocks, width = adj_ocean.shape
    kb = ocean_blocks.shape[1]
    entries = coast_cell.shape[0]
    chunks = entries // COUNT
    capr = 2 * entries // devices // LANES
    slots = devices * capr
    planes = STEPS + 1
    line = (chunks, 1, COUNT)
    vmem, anywhere = pl.BlockSpec(memory_space=pltpu.VMEM), pl.BlockSpec(memory_space=pl.ANY)
    return pl.pallas_call(
        step_kernel,
        out_shape=(
            jax.ShapeDtypeStruct((rows, cols), f32),
            jax.ShapeDtypeStruct((blocks, width), f32),
        ),
        in_specs=[anywhere] * 8 + [vmem] * 2,
        out_specs=(anywhere, vmem),
        scratch_shapes=[
            pltpu.VMEM((rows, cols), f32),
            pltpu.VMEM((rows, cols), f32),
            pltpu.VMEM((STEPS, rows, cols), jnp.int32),
            pltpu.VMEM(line, jnp.int32),
            pltpu.VMEM(line, jnp.int32),
            pltpu.VMEM(line, jnp.int32),
            pltpu.VMEM(line, f32),
            pltpu.VMEM(ocean_blocks.shape, bf16),
            pltpu.VMEM((rows + 2 * SUB, cols + 2 * LANES), f32),
            pltpu.VMEM((rows, cols), bf16),
            pltpu.VMEM((chunks, cols, COUNT), bf16),
            pltpu.VMEM(line, jnp.int32),
            pltpu.VMEM((chunks, slots, COUNT), bf16),
            pltpu.VMEM((chunks, LANES, COUNT), bf16),
            pltpu.VMEM((planes, devices, capr, LANES), f32),
            pltpu.VMEM((planes, devices, capr, LANES), f32),
            pltpu.VMEM((slots * LANES // COUNT, blocks, COUNT), bf16),
            pltpu.VMEM((slots * LANES // COUNT, LANES, COUNT), bf16),
            pltpu.VMEM((STEPS, 4, 1, max(rows, cols)), f32),
            pltpu.VMEM((STEPS, 4, 1, max(rows, cols)), f32),
            pltpu.VMEM((blocks, width), f32),
            pltpu.VMEM((kb * blocks, width), f32),
            pltpu.VMEM((group * blocks, kb * blocks), bf16),
            pltpu.VMEM((STEPS, group, blocks, width), f32),
            pltpu.VMEM((STEPS, group - 1, blocks, width), f32),
            pltpu.SemaphoreType.DMA((8 + STEPS - 1,)),
            pltpu.SemaphoreType.DMA((STEPS, 4)),
            pltpu.SemaphoreType.DMA((STEPS, 4)),
            pltpu.SemaphoreType.DMA((planes,)),
            pltpu.SemaphoreType.DMA((planes,)),
            pltpu.SemaphoreType.DMA((STEPS, group - 1)),
            pltpu.SemaphoreType.DMA((STEPS, group - 1)),
        ],
        compiler_params=pltpu.CompilerParams(
            vmem_limit_bytes=58 << 20, collective_id=0, has_side_effects=True
        ),
        name="adjoint_steps",
    )(
        adj_depth,
        conductance,
        wet,
        coast_cell.reshape(line),
        coast_dest.reshape(line),
        coast_node.reshape(line),
        coast_weight.reshape(line),
        ocean_blocks,
        ocean_target.T.reshape(1, -1),
        adj_ocean,
    )


def solution(mesh):
    in_specs = (
        P("land", "sea"),
        P("land", "sea"),
        P(None, "land", "sea"),
        P(("land", "sea")),
        P(("land", "sea"), None),
        P(("land", "sea")),
        P(("land", "sea")),
        P(("land", "sea"), None),
        P(("land", "sea"), None, None, None),
        P(("land", "sea"), None),
    )
    out_specs = (P("land", "sea"), P(("land", "sea"), None))
    return jax.shard_map(local, mesh=mesh, in_specs=in_specs, out_specs=out_specs, check_vma=False)
```

```python
import jax
import jax.numpy as jnp
from jax import lax
from jax.experimental import pallas as pl
from jax.experimental.pallas import tpu as pltpu
from jax.sharding import PartitionSpec as P

STEPS = 4
LANES = 128
SUB = 8
COUNT = 1024
PIECE = 256
SPAN = 512
BANDS = 4
MESH = pl.DeviceIdType.MESH
f32, bf16 = jnp.float32, jnp.bfloat16


def iota(shape, axis):
    return lax.broadcasted_iota(jnp.int32, shape, axis)


def halves(value):
    high = value.astype(bf16)
    return high, (value - high.astype(f32)).astype(bf16)


def across(a, b):
    return lax.dot_general(a, b, (((1,), (1,)), ((), ())), preferred_element_type=f32)


def one_hot(index, size):
    return jnp.where(iota((size, index.shape[1]), 0) == index, 1.0, 0.0).astype(bf16)


def beside_of(axis):
    count, me = lax.axis_size(axis), lax.axis_index(axis)
    return lax.rem(me + count - 1, count), lax.rem(me + 1, count)


def partner_of(index):
    seas = lax.axis_size("sea")
    return {"land": index // seas, "sea": lax.rem(index, seas)}


def step_kernel(
    table, depth_in, cond_in, wet_in, operator_in,
    cell_row, cell_col, slot, weight, nodes, target, adj, land_out, ocean_out,
    land, cond, wet, held,
    ext, masked, found, col_hot, slot_row, slot_lane, packs, got, node_row, node_lane,
    out_edge, in_edge, cur, terms, hot, summed, parts,
    loads, edge_sends, edge_recvs, pack_sends, pack_recvs, sends, recvs,
):
    group, sea = lax.axis_size("sea"), lax.axis_index("sea")
    lands, row_of = lax.axis_size("land"), lax.axis_index("land")
    devices, me = group * lands, row_of * group + sea
    rows, cols = land.shape
    blocks, width = adj.shape
    kb = held.shape[1]
    planes, capr = got.shape[0], got.shape[2]
    spans, got_chunks = cell_row.shape[0], node_row.shape[0]
    bands, band = masked.shape[0], masked.shape[1]
    lines = COUNT // LANES
    west, east = beside_of("sea")
    north, south = beside_of("land")

    pairs = [
        (depth_in, land), (wet_in.at[0], wet.at[0]), (cond_in, cond), (operator_in, held),
    ] + [(wet_in.at[t], wet.at[t]) for t in range(1, STEPS)]
    load = [pltpu.make_async_copy(a, b, loads.at[i]) for i, (a, b) in enumerate(pairs)]
    for copy in load:
        copy.start()

    barrier = pltpu.get_barrier_semaphore()

    def greet(d, _):
        to = partner_of(lax.rem(me + d, devices))
        pl.semaphore_signal(barrier, inc=1, device_id=to, device_id_type=MESH)
        return 0

    lax.fori_loop(1, devices, greet, 0)

    cur[...] = adj[...]
    for s in range(group):
        hot[s * blocks : (s + 1) * blocks, :] = one_hot(target[...] - s * blocks, blocks)
    others = [lax.rem(sea + d, group) for d in range(1, group)]

    def shares(t):
        return [
            pltpu.make_async_remote_copy(
                src_ref=summed.at[t, to],
                dst_ref=parts.at[t, i],
                send_sem=sends.at[t, i],
                recv_sem=recvs.at[t, i],
                device_id={"sea": to},
                device_id_type=MESH,
            )
            for i, to in enumerate(others)
        ]

    def step_terms(t):
        tall = 16
        sub = iota((tall, width), 0)
        for g in range(blocks // tall):
            own = cur[g * tall : (g + 1) * tall, :]
            wide = jnp.concatenate(
                [jnp.where(sub == j, own, 0.0).astype(bf16) for j in range(tall)], axis=1
            )
            for k in range(kb):
                block = held[g * tall : (g + 1) * tall, k].reshape(tall * width, width)
                terms[k * blocks + g * tall : k * blocks + (g + 1) * tall, :] = jnp.dot(
                    wide, block, preferred_element_type=f32
                )
        both = jnp.concatenate(halves(terms[...]), axis=1)
        total = jnp.dot(hot[...], both, preferred_element_type=f32)
        for s in range(group):
            part = total[s * blocks : (s + 1) * blocks]
            summed[t, s] = part[:, :width] + part[:, width:]
        for copy in shares(t):
            copy.start()

    def send_plane(p, slots):
        for d in range(packs.shape[1]):
            packs[p, d] = slots[d * capr : (d + 1) * capr]

        def send(d, _):
            index = lax.rem(me + d, devices)
            pltpu.make_async_remote_copy(
                src_ref=packs.at[p, index],
                dst_ref=got.at[p, me],
                send_sem=pack_sends.at[p],
                recv_sem=pack_recvs.at[p],
                device_id=partner_of(index),
                device_id_type=MESH,
            ).start()
            return 0

        lax.fori_loop(1, devices, send, 0)
        got[p, me] = packs[p, me]

    def arrived(p):
        pltpu.make_async_remote_copy(
            src_ref=packs.at[p, pl.ds(0, devices - 1)],
            dst_ref=got.at[p, pl.ds(0, devices - 1)],
            send_sem=pack_sends.at[p],
            recv_sem=pack_recvs.at[p],
            device_id=partner_of(lax.rem(me + 1, devices)),
            device_id_type=MESH,
        ).wait()

    def line(p, i):
        return jnp.concatenate(
            [got[p, i * lines // capr + k // capr, pl.ds(k % capr, 1), :] for k in range(lines)],
            axis=1,
        )

    def edges(t):
        return [
            pltpu.make_async_remote_copy(
                src_ref=out_edge.at[t, i],
                dst_ref=in_edge.at[t, i ^ 1],
                send_sem=edge_sends.at[t, i],
                recv_sem=edge_recvs.at[t, i ^ 1],
                device_id=to,
                device_id_type=MESH,
            )
            for i, to in enumerate(
                ({"land": north}, {"land": south}, {"sea": west}, {"sea": east})
            )
        ]

    def spread_of(t):
        masked_step = wet[t].astype(f32) * land[...]
        for b in range(bands):
            masked[b] = masked_step[b * band : (b + 1) * band].astype(bf16)
        ext[SUB : SUB + rows, LANES : LANES + cols] = cond[...] * masked_step
        first = ext[SUB : SUB + rows, LANES : 2 * LANES]
        last = ext[SUB : SUB + rows, cols : cols + LANES]
        sides = jnp.where(iota((rows, LANES), 1) < LANES // 2, first, last).T
        out_edge[t, 0] = ext[SUB : SUB + 1, LANES : LANES + cols]
        out_edge[t, 1] = ext[SUB + rows - 1 : SUB + rows, LANES : LANES + cols]
        out_edge[t, 2] = sides[0:1]
        out_edge[t, 3] = sides[LANES - 1 :]
        for copy in edges(t):
            copy.start()

    def land_step(t):
        for copy in edges(t):
            copy.wait()
        has = [jnp.where(c, 1.0, 0.0) for c in (row_of > 0, row_of < lands - 1, sea > 0, sea < group - 1)]
        ext[SUB - 1 : SUB, LANES : LANES + cols] = in_edge[t, 0] * has[0]
        ext[SUB + rows : SUB + rows + 1, LANES : LANES + cols] = in_edge[t, 1] * has[1]
        sub = iota((LANES, rows), 0)
        sides = jnp.where(
            sub == LANES - 1,
            in_edge[t, 2] * has[2],
            jnp.where(sub == 0, in_edge[t, 3] * has[3], 0.0),
        ).T
        ext[SUB : SUB + rows, 0:LANES] = sides
        ext[SUB : SUB + rows, LANES + cols :] = sides
        tall = min(rows, 128)
        for r in range(0, rows, tall):
            a = SUB + r
            spread = ext[a : a + tall, LANES : LANES + cols]
            beside = (
                ext[a - 1 : a - 1 + tall, LANES : LANES + cols]
                + ext[a + 1 : a + 1 + tall, LANES : LANES + cols]
                + ext[a : a + tall, LANES - 1 : LANES - 1 + cols]
                + ext[a : a + tall, LANES + 1 : LANES + 1 + cols]
            )
            land[r : r + tall] = land[r : r + tall] + (beside - 4.0 * spread)

    def index_span(i, _):
        col_hot[i] = one_hot(cell_col[i], cols)
        slot_row[i] = one_hot(slot[i] // LANES, slot_row.shape[1])
        slot_lane[i] = one_hot(slot[i] % LANES, LANES)
        return 0

    lax.fori_loop(0, spans, index_span, 0)
    pl.semaphore_wait(barrier, devices - 1)
    send_plane(planes - 1, nodes[...])

    def flux_plane(t):
        def pair(p, _):
            i, b = table[0, p], table[1, p]
            lines = jnp.dot(masked[b], col_hot[i], preferred_element_type=f32)
            here = iota((band, SPAN), 0) == cell_row[i] - b * band
            line = jnp.sum(jnp.where(here, lines, 0.0), axis=0, keepdims=True)
            found[...] += jnp.where(iota((spans, SPAN), 0) == i, line, 0.0)
            return 0

        found[...] = jnp.zeros_like(found)
        lax.fori_loop(0, spans + bands - 1, pair, 0, unroll=True)
        slots = jnp.zeros((slot_row.shape[1], LANES), f32)
        for i in range(spans):
            flux = (weight[i] * found[i : i + 1, :]).astype(bf16)
            slots = slots + across(slot_row[i], slot_lane[i] * flux)
        send_plane(t, slots)

    def node_hots():
        arrived(planes - 1)

        def chunk(i, _):
            place = line(planes - 1, i).astype(jnp.int32)
            node_row[i] = one_hot(place // LANES, blocks)
            node_lane[i] = one_hot(place % LANES, LANES)
            return 0

        lax.fori_loop(0, got_chunks, chunk, 0)

    def ocean_step(t):
        arrived(t)

        def chunk(i, acc):
            return acc + across(node_row[i], node_lane[i] * line(t, i).astype(bf16))

        coupled = lax.fori_loop(0, got_chunks, chunk, jnp.zeros((blocks, width), f32), unroll=True)
        result = 0.5 * cur[...] + coupled + summed[t, sea]
        for copy in shares(t):
            copy.wait()
        for i in range(group - 1):
            result = result + parts[t, i]
        cur[...] = result

    for copy in load[:3] + load[4:]:
        copy.wait()
    store = pltpu.make_async_copy(land, land_out, loads.at[0])

    def step(t, _):
        before, ahead = t > 0, t < STEPS

        @pl.when(before)
        def _():
            land_step(t - 1)

        @pl.when(ahead)
        def _():
            spread_of(t)
            flux_plane(t)

        @pl.when(t == STEPS)
        def _():
            store.start()

        @pl.when(before)
        def _():
            ocean_step(t - 1)

        @pl.when(t == 0)
        def _():
            load[3].wait()

        @pl.when(ahead)
        def _():
            step_terms(t)

        @pl.when(t == 0)
        def _():
            node_hots()

        return 0

    lax.fori_loop(0, STEPS + 1, step, 0)
    ocean_out[...] = cur[...]
    store.wait()


def index_kernel(
    cell, dest, node, weight,
    cell_row, cell_col, slot_out, weight_out, nodes_out, table,
    capacity, devices, rows, cols,
):
    chunks = cell.shape[0]
    spans, places = chunks * COUNT // SPAN, cell_row.shape[0]
    slots = nodes_out.shape[0]
    band = rows // BANDS * cols
    sub = iota((SUB, COUNT), 0)

    ends = jnp.zeros((SUB, 1), f32)
    for i in range(chunks):
        ends = ends + jnp.sum(jnp.where(cell[i] // band <= sub, 1.0, 0.0), axis=1, keepdims=True)
    starts = jnp.zeros((SUB, 1), f32)
    for i in range(chunks):
        starts = starts + jnp.sum(jnp.where(cell[i] // band < sub, 1.0, 0.0), axis=1, keepdims=True)

    triangle = jnp.where(iota((PIECE, PIECE), 0) <= iota((PIECE, PIECE), 1), 1.0, 0.0).astype(bf16)

    def digits(values, hot):
        return [hot * v.astype(f32).astype(bf16) for v in values]

    def chunk(i, carry):
        base, found, nodes = carry
        dest_now, place, node_now = dest[i], cell[i], node[i]
        matches = jnp.concatenate(
            [
                jnp.where(iota((devices, COUNT), 0) == dest_now, 1.0, 0.0),
                jnp.where(sub == place // band, 1.0, 0.0),
            ],
            axis=0,
        )
        ranks, orders = [], []
        for p in range(0, COUNT, PIECE):
            own = matches[:, p : p + PIECE]
            running = jnp.dot(own.astype(bf16), triangle, preferred_element_type=f32)
            counted = own * (running + base)
            ranks.append(jnp.sum(counted[:devices], axis=0, keepdims=True))
            orders.append(jnp.sum(counted[devices:], axis=0, keepdims=True))
            base = base + jnp.sum(own, axis=1, keepdims=True)
        slot = dest_now * capacity + jnp.concatenate(ranks, axis=1).astype(jnp.int32) - 1
        order = jnp.concatenate(orders, axis=1).astype(jnp.int32) - 1
        hot = one_hot(order % LANES, LANES)
        high, low = halves(weight[i])
        parts = digits(
            (place // 65536, place // 256 % 256, place % 256, slot // 256, slot % 256), hot
        ) + [hot * high, hot * low]
        found = found + across(one_hot(order // LANES, places), jnp.concatenate(parts, axis=0))
        parts = digits((node_now // LANES, node_now % LANES), one_hot(slot % LANES, LANES))
        nodes = nodes + across(one_hot(slot // LANES, slots), jnp.concatenate(parts, axis=0))
        return base, found, nodes

    base = jnp.concatenate([jnp.zeros((devices, 1), f32), starts], axis=0)
    _, found, nodes = lax.fori_loop(
        0,
        chunks,
        chunk,
        (base, jnp.zeros((places, 7 * LANES), f32), jnp.zeros((slots, 2 * LANES), f32)),
    )
    part = [found[:, k * LANES : (k + 1) * LANES] for k in range(7)]
    place = (part[0] * 65536.0 + part[1] * 256.0 + part[2]).astype(jnp.int32)
    cell_row[...] = place // cols
    cell_col[...] = place % cols
    slot_out[...] = (part[3] * 256.0 + part[4]).astype(jnp.int32)
    weight_out[...] = part[5] + part[6]
    nodes_out[...] = nodes[:, :LANES] * float(LANES) + nodes[:, LANES:]

    band_of = iota((SUB, LANES), 0)
    last = jnp.maximum((ends.astype(jnp.int32) + SPAN - 1) // SPAN - 1, 0)
    down = (last + band_of < iota((SUB, LANES), 1)) & (band_of < BANDS - 1)
    bands = jnp.sum(jnp.where(down, 1.0, 0.0), axis=0, keepdims=True).astype(jnp.int32)
    spans_of = iota((1, LANES), 1) - bands
    spans_of = jnp.minimum(spans_of, spans - 1)
    table[...] = jnp.where(band_of == 0, spans_of, bands)


def sorted_entries(cell, dest, node, weight, capr, devices, rows, cols):
    entries = cell.shape[0]
    line = (entries // COUNT, 1, COUNT)
    places = entries // LANES
    vmem = pl.BlockSpec(memory_space=pltpu.VMEM)
    whole = jax.ShapeDtypeStruct((places, LANES), jnp.int32)

    def kernel(*refs):
        index_kernel(*refs, capr * LANES, devices, rows, cols)

    *sorted_, nodes, table = pl.pallas_call(
        kernel,
        out_shape=(
            whole,
            whole,
            whole,
            jax.ShapeDtypeStruct((places, LANES), f32),
            jax.ShapeDtypeStruct((devices * capr, LANES), f32),
            jax.ShapeDtypeStruct((SUB, LANES), jnp.int32),
        ),
        in_specs=[vmem] * 4,
        out_specs=(vmem,) * 6,
        compiler_params=pltpu.CompilerParams(vmem_limit_bytes=58 << 20),
        name="coast_index",
    )(cell.reshape(line), dest.reshape(line), node.reshape(line), weight.reshape(line))
    span = (entries // SPAN, 1, SPAN)
    return [v.reshape(span) for v in sorted_], nodes, table


def finish_kernel(land, ocean, land_out, ocean_out, held, kept, sems):
    rows, tall = land.shape[0], land.shape[0] // 4
    moves = [(land.at[pl.ds(r, tall)], held.at[pl.ds(r, tall)], land_out.at[pl.ds(r, tall)]) for r in range(0, rows, tall)]
    moves.append((ocean, kept, ocean_out))
    into = [pltpu.make_async_copy(a, b, sems.at[0, i]) for i, (a, b, _) in enumerate(moves)]
    out = [pltpu.make_async_copy(b, c, sems.at[1, i]) for i, (_, b, c) in enumerate(moves)]
    for copy in into:
        copy.start()
    for first, second in zip(into, out):
        first.wait()
        second.start()
    for copy in out:
        copy.wait()


def finish(land, ocean):
    anywhere = pl.BlockSpec(memory_space=pl.ANY)
    return tuple(
        pl.pallas_call(
            finish_kernel,
            out_shape=(
                jax.ShapeDtypeStruct(land.shape, f32),
                jax.ShapeDtypeStruct(ocean.shape, f32),
            ),
            in_specs=[anywhere] * 2,
            out_specs=(anywhere, anywhere),
            scratch_shapes=[
                pltpu.VMEM(land.shape, f32),
                pltpu.VMEM(ocean.shape, f32),
                pltpu.SemaphoreType.DMA((2, 5)),
            ],
            name="results",
        )(land, ocean)
    )


def local(
    adj_depth,
    conductance,
    wet,
    coast_cell,
    coast_dest,
    coast_node,
    coast_weight,
    adj_ocean,
    ocean_blocks,
    ocean_target,
):
    group, devices = lax.axis_size("sea"), lax.axis_size(("land", "sea"))
    rows, cols = adj_depth.shape
    blocks, width = adj_ocean.shape
    kb = ocean_blocks.shape[1]
    entries = coast_cell.shape[0]
    capr = 2 * entries // devices // LANES
    slots = devices * capr
    planes = STEPS + 1
    spans = entries // SPAN
    entries_sorted, nodes, table = sorted_entries(
        coast_cell, coast_dest, coast_node, coast_weight, capr, devices, rows, cols
    )
    vmem, anywhere = pl.BlockSpec(memory_space=pltpu.VMEM), pl.BlockSpec(memory_space=pl.ANY)
    land, ocean = pl.pallas_call(
        step_kernel,
        out_shape=(
            jax.ShapeDtypeStruct((rows, cols), f32),
            jax.ShapeDtypeStruct((blocks, width), f32),
        ),
        in_specs=[pl.BlockSpec(memory_space=pltpu.SMEM)] + [anywhere] * 4 + [vmem] * 7,
        out_specs=(anywhere, vmem),
        scratch_shapes=[
            pltpu.VMEM((rows, cols), f32),
            pltpu.VMEM((rows, cols), f32),
            pltpu.VMEM((STEPS, rows, cols), jnp.int32),
            pltpu.VMEM(ocean_blocks.shape, bf16),
            pltpu.VMEM((rows + 2 * SUB, cols + 2 * LANES), f32),
            pltpu.VMEM((BANDS, rows // BANDS, cols), bf16),
            pltpu.VMEM((spans, SPAN), f32),
            pltpu.VMEM((spans, cols, SPAN), bf16),
            pltpu.VMEM((spans, slots, SPAN), bf16),
            pltpu.VMEM((spans, LANES, SPAN), bf16),
            pltpu.VMEM((planes, devices, capr, LANES), f32),
            pltpu.VMEM((planes, devices, capr, LANES), f32),
            pltpu.VMEM((slots * LANES // COUNT, blocks, COUNT), bf16),
            pltpu.VMEM((slots * LANES // COUNT, LANES, COUNT), bf16),
            pltpu.VMEM((STEPS, 4, 1, max(rows, cols)), f32),
            pltpu.VMEM((STEPS, 4, 1, max(rows, cols)), f32),
            pltpu.VMEM((blocks, width), f32),
            pltpu.VMEM((kb * blocks, width), f32),
            pltpu.VMEM((group * blocks, kb * blocks), bf16),
            pltpu.VMEM((STEPS, group, blocks, width), f32),
            pltpu.VMEM((STEPS, group - 1, blocks, width), f32),
            pltpu.SemaphoreType.DMA((4 + STEPS - 1,)),
            pltpu.SemaphoreType.DMA((STEPS, 4)),
            pltpu.SemaphoreType.DMA((STEPS, 4)),
            pltpu.SemaphoreType.DMA((planes,)),
            pltpu.SemaphoreType.DMA((planes,)),
            pltpu.SemaphoreType.DMA((STEPS, group - 1)),
            pltpu.SemaphoreType.DMA((STEPS, group - 1)),
        ],
        compiler_params=pltpu.CompilerParams(
            vmem_limit_bytes=58 << 20, collective_id=0, has_side_effects=True
        ),
        name="adjoint_steps",
    )(
        table,
        adj_depth,
        conductance,
        wet,
        ocean_blocks,
        *entries_sorted,
        nodes,
        ocean_target.T.reshape(1, -1),
        adj_ocean,
    )
    return finish(land, ocean)


def solution(mesh):
    in_specs = (
        P("land", "sea"),
        P("land", "sea"),
        P(None, "land", "sea"),
        P(("land", "sea")),
        P(("land", "sea"), None),
        P(("land", "sea")),
        P(("land", "sea")),
        P(("land", "sea"), None),
        P(("land", "sea"), None, None, None),
        P(("land", "sea"), None),
    )
    out_specs = (P("land", "sea"), P(("land", "sea"), None))
    return jax.shard_map(local, mesh=mesh, in_specs=in_specs, out_specs=out_specs, check_vma=False)
```

```python
import jax
import jax.numpy as jnp
from jax import lax
from jax.experimental import pallas as pl
from jax.experimental.pallas import tpu as pltpu
from jax.sharding import PartitionSpec as P

STEPS = 4
LANES = 128
SUB = 8
COUNT = 1024
PIECE = 256
SPAN = 512
BANDS = 4
UNROLL = True
MESH = pl.DeviceIdType.MESH
f32, bf16 = jnp.float32, jnp.bfloat16


def iota(shape, axis):
    return lax.broadcasted_iota(jnp.int32, shape, axis)


def halves(value):
    high = value.astype(bf16)
    return high, (value - high.astype(f32)).astype(bf16)


def across(a, b):
    return lax.dot_general(a, b, (((1,), (1,)), ((), ())), preferred_element_type=f32)


def one_hot(index, size):
    parts = []
    for first in range(0, size, 256):
        at = iota((min(256, size - first), index.shape[1]), 0).astype(f32).astype(bf16)
        here = at == (index - first).astype(f32).astype(bf16)
        parts.append(jnp.where(here, jnp.ones((), bf16), jnp.zeros((), bf16)))
    return parts[0] if len(parts) == 1 else jnp.concatenate(parts, axis=0)


def beside_of(axis):
    count, me = lax.axis_size(axis), lax.axis_index(axis)
    return lax.rem(me + count - 1, count), lax.rem(me + 1, count)


def partner_of(index):
    seas = lax.axis_size("sea")
    return {"land": index // seas, "sea": lax.rem(index, seas)}


def index_entries(cell, dest, node, weight_of, sorted_to, meeting, capr, devices, rows, cols):
    chunks = cell.shape[0]
    spans, places = chunks * COUNT // SPAN, chunks * COUNT // LANES
    capacity, slots = capr * LANES, devices * capr
    band = rows // BANDS * cols
    sub = iota((SUB, COUNT), 0)

    ends = starts = jnp.zeros((SUB, COUNT), f32)
    for i in range(chunks):
        at = cell[i] // band
        ends = ends + jnp.where(at <= sub, 1.0, 0.0)
        starts = starts + jnp.where(at < sub, 1.0, 0.0)
    ends = jnp.sum(ends, axis=1, keepdims=True)
    starts = jnp.sum(starts, axis=1, keepdims=True)

    triangle = jnp.where(iota((PIECE, PIECE), 0) <= iota((PIECE, PIECE), 1), 1.0, 0.0).astype(bf16)

    def digits(values, hot):
        return [hot * v.astype(f32).astype(bf16) for v in values]

    def chunk(i, carry):
        base, found, nodes = carry
        dest_now, place, node_now = dest[i], cell[i], node[i]
        matches = jnp.concatenate(
            [
                jnp.where(iota((devices, COUNT), 0) == dest_now, 1.0, 0.0),
                jnp.where(sub == place // band, 1.0, 0.0),
            ],
            axis=0,
        )
        ranks, orders = [], []
        for p in range(0, COUNT, PIECE):
            own = matches[:, p : p + PIECE]
            running = jnp.dot(own.astype(bf16), triangle, preferred_element_type=f32)
            counted = own * (running + base)
            ranks.append(jnp.sum(counted[:devices], axis=0, keepdims=True))
            orders.append(jnp.sum(counted[devices:], axis=0, keepdims=True))
            base = base + jnp.sum(own, axis=1, keepdims=True)
        slot = dest_now * capacity + jnp.concatenate(ranks, axis=1).astype(jnp.int32) - 1
        order = jnp.concatenate(orders, axis=1).astype(jnp.int32) - 1
        hot = one_hot(order % LANES, LANES)
        high, low = halves(weight_of[i])
        parts = digits(
            (place // 65536, place // 256 % 256, place % 256, slot // 256, slot % 256), hot
        ) + [hot * high, hot * low]
        found = found + across(one_hot(order // LANES, places), jnp.concatenate(parts, axis=0))
        parts = digits((node_now // LANES, node_now % LANES), one_hot(slot % LANES, LANES))
        nodes = nodes + across(one_hot(slot // LANES, slots), jnp.concatenate(parts, axis=0))
        return base, found, nodes

    base = jnp.concatenate([jnp.zeros((devices, 1), f32), starts], axis=0)
    _, found, nodes = lax.fori_loop(
        0,
        chunks,
        chunk,
        (base, jnp.zeros((places, 7 * LANES), f32), jnp.zeros((slots, 2 * LANES), f32)),
        unroll=UNROLL,
    )
    part = [found[:, k * LANES : (k + 1) * LANES] for k in range(7)]
    place = (part[0] * 65536.0 + part[1] * 256.0 + part[2]).astype(jnp.int32)
    values = (
        place // cols,
        place % cols,
        (part[3] * 256.0 + part[4]).astype(jnp.int32),
        part[5] + part[6],
    )
    per = SPAN // LANES
    for to, value in zip(sorted_to, values):
        for i in range(spans):
            to[i] = jnp.concatenate([value[i * per + k : i * per + k + 1] for k in range(per)], axis=1)

    band_of = iota((SUB, LANES), 0)
    last = jnp.maximum((ends.astype(jnp.int32) + SPAN - 1) // SPAN - 1, 0)
    down = (last + band_of < iota((SUB, LANES), 1)) & (band_of < BANDS - 1)
    bands = jnp.sum(jnp.where(down, 1.0, 0.0), axis=0, keepdims=True).astype(jnp.int32)
    spans_of = jnp.minimum(iota((1, LANES), 1) - bands, spans - 1)
    meeting[...] = jnp.where(band_of == 0, spans_of, bands)
    return nodes[:, :LANES] * float(LANES) + nodes[:, LANES:]


def step_kernel(
    cell_in, dest_in, node_in, weight_in, depth_in, cond_in, wet_in, operator_in,
    target, adj, land_out, ocean_out,
    cell, dest, node, weight_of, cell_row, cell_col, slot, weight, meeting, table,
    land, cond, wet, held,
    ext, masked, found, col_hot, slot_row, slot_lane, packs, got, node_row, node_lane,
    out_edge, in_edge, cur, terms, hot, summed, parts,
    loads, edge_sends, edge_recvs, pack_sends, pack_recvs, sends, recvs,
):
    group, sea = lax.axis_size("sea"), lax.axis_index("sea")
    lands, row_of = lax.axis_size("land"), lax.axis_index("land")
    devices, me = group * lands, row_of * group + sea
    rows, cols = land.shape
    blocks, width = adj.shape
    kb = held.shape[1]
    planes, capr = got.shape[0], got.shape[2]
    spans, got_chunks = cell_row.shape[0], node_row.shape[0]
    bands, band = masked.shape[0], masked.shape[1]
    lines = COUNT // LANES
    west, east = beside_of("sea")
    north, south = beside_of("land")

    pairs = [
        (cell_in, cell), (dest_in, dest), (node_in, node), (weight_in, weight_of),
        (operator_in, held), (depth_in, land), (wet_in.at[0], wet.at[0]), (cond_in, cond),
    ] + [(wet_in.at[t], wet.at[t]) for t in range(1, STEPS)]
    load = [pltpu.make_async_copy(a, b, loads.at[i]) for i, (a, b) in enumerate(pairs)]
    for copy in load:
        copy.start()

    barrier = pltpu.get_barrier_semaphore()

    def greet(d, _):
        to = partner_of(lax.rem(me + d, devices))
        pl.semaphore_signal(barrier, inc=1, device_id=to, device_id_type=MESH)
        return 0

    lax.fori_loop(1, devices, greet, 0)

    cur[...] = adj[...]
    for s in range(group):
        hot[s * blocks : (s + 1) * blocks, :] = one_hot(target[...] - s * blocks, blocks)
    others = [lax.rem(sea + d, group) for d in range(1, group)]

    def shares(t):
        return [
            pltpu.make_async_remote_copy(
                src_ref=summed.at[t, to],
                dst_ref=parts.at[t, i],
                send_sem=sends.at[t, i],
                recv_sem=recvs.at[t, i],
                device_id={"sea": to},
                device_id_type=MESH,
            )
            for i, to in enumerate(others)
        ]

    def step_terms(t):
        tall = 16
        sub = iota((tall, width), 0)
        for g in range(blocks // tall):
            own = cur[g * tall : (g + 1) * tall, :]
            wide = jnp.concatenate(
                [jnp.where(sub == j, own, 0.0).astype(bf16) for j in range(tall)], axis=1
            )
            for k in range(kb):
                block = held[g * tall : (g + 1) * tall, k].reshape(tall * width, width)
                terms[k * blocks + g * tall : k * blocks + (g + 1) * tall, :] = jnp.dot(
                    wide, block, preferred_element_type=f32
                )
        both = jnp.concatenate(halves(terms[...]), axis=1)
        total = jnp.dot(hot[...], both, preferred_element_type=f32)
        for s in range(group):
            part = total[s * blocks : (s + 1) * blocks]
            summed[t, s] = part[:, :width] + part[:, width:]
        for copy in shares(t):
            copy.start()

    def send_plane(p, slots):
        for d in range(packs.shape[1]):
            packs[p, d] = slots[d * capr : (d + 1) * capr]

        def send(d, _):
            index = lax.rem(me + d, devices)
            pltpu.make_async_remote_copy(
                src_ref=packs.at[p, index],
                dst_ref=got.at[p, me],
                send_sem=pack_sends.at[p],
                recv_sem=pack_recvs.at[p],
                device_id=partner_of(index),
                device_id_type=MESH,
            ).start()
            return 0

        lax.fori_loop(1, devices, send, 0)
        got[p, me] = packs[p, me]

    def arrived(p):
        pltpu.make_async_remote_copy(
            src_ref=packs.at[p, pl.ds(0, devices - 1)],
            dst_ref=got.at[p, pl.ds(0, devices - 1)],
            send_sem=pack_sends.at[p],
            recv_sem=pack_recvs.at[p],
            device_id=partner_of(lax.rem(me + 1, devices)),
            device_id_type=MESH,
        ).wait()

    def line(p, i):
        return jnp.concatenate(
            [got[p, i * lines // capr + k // capr, pl.ds(k % capr, 1), :] for k in range(lines)],
            axis=1,
        )

    def edges(t):
        return [
            pltpu.make_async_remote_copy(
                src_ref=out_edge.at[t, i],
                dst_ref=in_edge.at[t, i ^ 1],
                send_sem=edge_sends.at[t, i],
                recv_sem=edge_recvs.at[t, i ^ 1],
                device_id=to,
                device_id_type=MESH,
            )
            for i, to in enumerate(
                ({"land": north}, {"land": south}, {"sea": west}, {"sea": east})
            )
        ]

    def spread_of(t):
        masked_step = wet[t].astype(f32) * land[...]
        for b in range(bands):
            masked[b] = masked_step[b * band : (b + 1) * band].astype(bf16)
        ext[SUB : SUB + rows, LANES : LANES + cols] = cond[...] * masked_step
        first = ext[SUB : SUB + rows, LANES : 2 * LANES]
        last = ext[SUB : SUB + rows, cols : cols + LANES]
        sides = jnp.where(iota((rows, LANES), 1) < LANES // 2, first, last).T
        out_edge[t, 0] = ext[SUB : SUB + 1, LANES : LANES + cols]
        out_edge[t, 1] = ext[SUB + rows - 1 : SUB + rows, LANES : LANES + cols]
        out_edge[t, 2] = sides[0:1]
        out_edge[t, 3] = sides[LANES - 1 :]
        for copy in edges(t):
            copy.start()

    def land_step(t):
        for copy in edges(t):
            copy.wait()
        has = [jnp.where(c, 1.0, 0.0) for c in (row_of > 0, row_of < lands - 1, sea > 0, sea < group - 1)]
        ext[SUB - 1 : SUB, LANES : LANES + cols] = in_edge[t, 0] * has[0]
        ext[SUB + rows : SUB + rows + 1, LANES : LANES + cols] = in_edge[t, 1] * has[1]
        sub = iota((LANES, rows), 0)
        sides = jnp.where(
            sub == LANES - 1,
            in_edge[t, 2] * has[2],
            jnp.where(sub == 0, in_edge[t, 3] * has[3], 0.0),
        ).T
        ext[SUB : SUB + rows, 0:LANES] = sides
        ext[SUB : SUB + rows, LANES + cols :] = sides
        tall = min(rows, 128)
        for r in range(0, rows, tall):
            a = SUB + r
            spread = ext[a : a + tall, LANES : LANES + cols]
            beside = (
                ext[a - 1 : a - 1 + tall, LANES : LANES + cols]
                + ext[a + 1 : a + 1 + tall, LANES : LANES + cols]
                + ext[a : a + tall, LANES - 1 : LANES - 1 + cols]
                + ext[a : a + tall, LANES + 1 : LANES + 1 + cols]
            )
            land[r : r + tall] = land[r : r + tall] + (beside - 4.0 * spread)

    for copy in load[:4]:
        copy.wait()
    nodes = index_entries(
        cell, dest, node, weight_of, (cell_row, cell_col, slot, weight), meeting,
        capr, devices, rows, cols,
    )
    into_scalars = pltpu.make_async_copy(meeting, table, loads.at[0])
    into_scalars.start()
    pl.semaphore_wait(barrier, devices - 1)
    send_plane(planes - 1, nodes)
    load[4].wait()
    step_terms(0)

    def index_span(i, _):
        col_hot[i] = one_hot(cell_col[i], cols)
        slot_row[i] = one_hot(slot[i] // LANES, slot_row.shape[1])
        slot_lane[i] = one_hot(slot[i] % LANES, LANES)
        return 0

    lax.fori_loop(0, spans, index_span, 0)
    into_scalars.wait()

    def flux_plane(t):
        def pair(p, _):
            i = jnp.clip(table[0, p], 0, spans - 1)
            b = jnp.clip(table[1, p], 0, bands - 1)
            lines = jnp.dot(masked[b], col_hot[i], preferred_element_type=f32)
            here = iota((band, SPAN), 0) == cell_row[i] - b * band
            line = jnp.sum(jnp.where(here, lines, 0.0), axis=0, keepdims=True)
            found[...] += jnp.where(iota((spans, SPAN), 0) == i, line, 0.0)
            return 0

        found[...] = jnp.zeros_like(found)
        lax.fori_loop(0, spans + bands - 1, pair, 0, unroll=True)
        slots = jnp.zeros((slot_row.shape[1], LANES), f32)
        for i in range(spans):
            flux = (weight[i] * found[i : i + 1, :]).astype(bf16)
            slots = slots + across(slot_row[i], slot_lane[i] * flux)
        send_plane(t, slots)

    def node_hots():
        arrived(planes - 1)

        def chunk(i, _):
            place = line(planes - 1, i).astype(jnp.int32)
            node_row[i] = one_hot(place // LANES, blocks)
            node_lane[i] = one_hot(place % LANES, LANES)
            return 0

        lax.fori_loop(0, got_chunks, chunk, 0)

    def ocean_step(t):
        arrived(t)

        def chunk(i, acc):
            return acc + across(node_row[i], node_lane[i] * line(t, i).astype(bf16))

        coupled = lax.fori_loop(0, got_chunks, chunk, jnp.zeros((blocks, width), f32), unroll=True)
        result = 0.5 * cur[...] + coupled + summed[t, sea]
        for copy in shares(t):
            copy.wait()
        for i in range(group - 1):
            result = result + parts[t, i]
        cur[...] = result

    for copy in load[5:]:
        copy.wait()
    store = pltpu.make_async_copy(land, land_out, loads.at[0])

    def step(t, _):
        before, ahead = t > 0, t < STEPS

        @pl.when(before)
        def _():
            land_step(t - 1)

        @pl.when(ahead)
        def _():
            spread_of(t)
            flux_plane(t)

        @pl.when(t == STEPS)
        def _():
            store.start()

        @pl.when(before)
        def _():
            ocean_step(t - 1)

        @pl.when(before & ahead)
        def _():
            step_terms(t)

        @pl.when(t == 0)
        def _():
            node_hots()

        return 0

    lax.fori_loop(0, STEPS + 1, step, 0)
    ocean_out[...] = cur[...]
    store.wait()


def finish_kernel(land, ocean, land_out, ocean_out, held, kept, sems):
    rows, tall = land.shape[0], land.shape[0] // 4
    moves = [(land.at[pl.ds(r, tall)], held.at[pl.ds(r, tall)], land_out.at[pl.ds(r, tall)]) for r in range(0, rows, tall)]
    moves.append((ocean, kept, ocean_out))
    into = [pltpu.make_async_copy(a, b, sems.at[0, i]) for i, (a, b, _) in enumerate(moves)]
    out = [pltpu.make_async_copy(b, c, sems.at[1, i]) for i, (_, b, c) in enumerate(moves)]
    for copy in into:
        copy.start()
    for first, second in zip(into, out):
        first.wait()
        second.start()
    for copy in out:
        copy.wait()


def finish(land, ocean):
    anywhere = pl.BlockSpec(memory_space=pl.ANY)
    return tuple(
        pl.pallas_call(
            finish_kernel,
            out_shape=(
                jax.ShapeDtypeStruct(land.shape, f32),
                jax.ShapeDtypeStruct(ocean.shape, f32),
            ),
            in_specs=[anywhere] * 2,
            out_specs=(anywhere, anywhere),
            scratch_shapes=[
                pltpu.VMEM(land.shape, f32),
                pltpu.VMEM(ocean.shape, f32),
                pltpu.SemaphoreType.DMA((2, 5)),
            ],
            name="results",
        )(land, ocean)
    )


def local(
    adj_depth,
    conductance,
    wet,
    coast_cell,
    coast_dest,
    coast_node,
    coast_weight,
    adj_ocean,
    ocean_blocks,
    ocean_target,
):
    group, devices = lax.axis_size("sea"), lax.axis_size(("land", "sea"))
    rows, cols = adj_depth.shape
    blocks, width = adj_ocean.shape
    kb = ocean_blocks.shape[1]
    entries = coast_cell.shape[0]
    capr = 2 * entries // devices // LANES
    slots = devices * capr
    planes = STEPS + 1
    line, span = (entries // COUNT, 1, COUNT), (entries // SPAN, 1, SPAN)
    spans = span[0]
    vmem, anywhere = pl.BlockSpec(memory_space=pltpu.VMEM), pl.BlockSpec(memory_space=pl.ANY)
    land, ocean = pl.pallas_call(
        step_kernel,
        out_shape=(
            jax.ShapeDtypeStruct((rows, cols), f32),
            jax.ShapeDtypeStruct((blocks, width), f32),
        ),
        in_specs=[anywhere] * 8 + [vmem] * 2,
        out_specs=(anywhere, vmem),
        scratch_shapes=[
            pltpu.VMEM(line, jnp.int32),
            pltpu.VMEM(line, jnp.int32),
            pltpu.VMEM(line, jnp.int32),
            pltpu.VMEM(line, f32),
            pltpu.VMEM(span, jnp.int32),
            pltpu.VMEM(span, jnp.int32),
            pltpu.VMEM(span, jnp.int32),
            pltpu.VMEM(span, f32),
            pltpu.VMEM((SUB, LANES), jnp.int32),
            pltpu.SMEM((SUB, LANES), jnp.int32),
            pltpu.VMEM((rows, cols), f32),
            pltpu.VMEM((rows, cols), f32),
            pltpu.VMEM((STEPS, rows, cols), jnp.int32),
            pltpu.VMEM(ocean_blocks.shape, bf16),
            pltpu.VMEM((rows + 2 * SUB, cols + 2 * LANES), f32),
            pltpu.VMEM((BANDS, rows // BANDS, cols), bf16),
            pltpu.VMEM((spans, SPAN), f32),
            pltpu.VMEM((spans, cols, SPAN), bf16),
            pltpu.VMEM((spans, slots, SPAN), bf16),
            pltpu.VMEM((spans, LANES, SPAN), bf16),
            pltpu.VMEM((planes, devices, capr, LANES), f32),
            pltpu.VMEM((planes, devices, capr, LANES), f32),
            pltpu.VMEM((slots * LANES // COUNT, blocks, COUNT), bf16),
            pltpu.VMEM((slots * LANES // COUNT, LANES, COUNT), bf16),
            pltpu.VMEM((STEPS, 4, 1, max(rows, cols)), f32),
            pltpu.VMEM((STEPS, 4, 1, max(rows, cols)), f32),
            pltpu.VMEM((blocks, width), f32),
            pltpu.VMEM((kb * blocks, width), f32),
            pltpu.VMEM((group * blocks, kb * blocks), bf16),
            pltpu.VMEM((STEPS, group, blocks, width), f32),
            pltpu.VMEM((STEPS, group - 1, blocks, width), f32),
            pltpu.SemaphoreType.DMA((8 + STEPS - 1,)),
            pltpu.SemaphoreType.DMA((STEPS, 4)),
            pltpu.SemaphoreType.DMA((STEPS, 4)),
            pltpu.SemaphoreType.DMA((planes,)),
            pltpu.SemaphoreType.DMA((planes,)),
            pltpu.SemaphoreType.DMA((STEPS, group - 1)),
            pltpu.SemaphoreType.DMA((STEPS, group - 1)),
        ],
        compiler_params=pltpu.CompilerParams(
            vmem_limit_bytes=58 << 20, collective_id=0, has_side_effects=True
        ),
        name="adjoint_steps",
    )(
        coast_cell.reshape(line),
        coast_dest.reshape(line),
        coast_node.reshape(line),
        coast_weight.reshape(line),
        adj_depth,
        conductance,
        wet,
        ocean_blocks,
        ocean_target.T.reshape(1, -1),
        adj_ocean,
    )
    return finish(land, ocean)


def solution(mesh):
    in_specs = (
        P("land", "sea"),
        P("land", "sea"),
        P(None, "land", "sea"),
        P(("land", "sea")),
        P(("land", "sea"), None),
        P(("land", "sea")),
        P(("land", "sea")),
        P(("land", "sea"), None),
        P(("land", "sea"), None, None, None),
        P(("land", "sea"), None),
    )
    out_specs = (P("land", "sea"), P(("land", "sea"), None))
    return jax.shard_map(local, mesh=mesh, in_specs=in_specs, out_specs=out_specs, check_vma=False)
```

```python
import jax
import jax.numpy as jnp
from jax import lax
from jax.experimental import pallas as pl
from jax.experimental.pallas import tpu as pltpu
from jax.sharding import PartitionSpec as P

STEPS = 4
LANES = 128
SUB = 8
COUNT = 1024
PIECE = 256
SPAN = 512
BANDS = 4
UNROLL = True
MESH = pl.DeviceIdType.MESH
f32, bf16 = jnp.float32, jnp.bfloat16


def iota(shape, axis):
    return lax.broadcasted_iota(jnp.int32, shape, axis)


def halves(value):
    high = value.astype(bf16)
    return high, (value - high.astype(f32)).astype(bf16)


def across(a, b):
    return lax.dot_general(a, b, (((1,), (1,)), ((), ())), preferred_element_type=f32)


def one_hot(index, size):
    parts = []
    for first in range(0, size, 256):
        at = iota((min(256, size - first), index.shape[1]), 0).astype(f32).astype(bf16)
        here = at == (index - first).astype(f32).astype(bf16)
        parts.append(jnp.where(here, jnp.ones((), bf16), jnp.zeros((), bf16)))
    return parts[0] if len(parts) == 1 else jnp.concatenate(parts, axis=0)


def beside_of(axis):
    count, me = lax.axis_size(axis), lax.axis_index(axis)
    return lax.rem(me + count - 1, count), lax.rem(me + 1, count)


def partner_of(index):
    seas = lax.axis_size("sea")
    return {"land": index // seas, "sea": lax.rem(index, seas)}


def index_entries(cell, dest, node, weight_of, sorted_to, meeting, capr, devices, rows, cols):
    chunks = cell.shape[0]
    spans, places = chunks * COUNT // SPAN, chunks * COUNT // LANES
    capacity, slots = capr * LANES, devices * capr
    band = rows // BANDS * cols
    sub = iota((SUB, COUNT), 0)

    ends = starts = jnp.zeros((SUB, COUNT), f32)
    for i in range(chunks):
        at = cell[i] // band
        ends = ends + jnp.where(at <= sub, 1.0, 0.0)
        starts = starts + jnp.where(at < sub, 1.0, 0.0)
    ends = jnp.sum(ends, axis=1, keepdims=True)
    starts = jnp.sum(starts, axis=1, keepdims=True)

    triangle = jnp.where(iota((PIECE, PIECE), 0) <= iota((PIECE, PIECE), 1), 1.0, 0.0).astype(bf16)

    def digits(values, hot):
        return [hot * v.astype(f32).astype(bf16) for v in values]

    def chunk(i, carry):
        base, found, nodes = carry
        dest_now, place, node_now = dest[i], cell[i], node[i]
        matches = jnp.concatenate(
            [
                jnp.where(iota((devices, COUNT), 0) == dest_now, 1.0, 0.0),
                jnp.where(sub == place // band, 1.0, 0.0),
            ],
            axis=0,
        )
        ranks, orders = [], []
        for p in range(0, COUNT, PIECE):
            own = matches[:, p : p + PIECE]
            running = jnp.dot(own.astype(bf16), triangle, preferred_element_type=f32)
            counted = own * (running + base)
            ranks.append(jnp.sum(counted[:devices], axis=0, keepdims=True))
            orders.append(jnp.sum(counted[devices:], axis=0, keepdims=True))
            base = base + jnp.sum(own, axis=1, keepdims=True)
        slot = dest_now * capacity + jnp.concatenate(ranks, axis=1).astype(jnp.int32) - 1
        order = jnp.concatenate(orders, axis=1).astype(jnp.int32) - 1
        hot = one_hot(order % LANES, LANES)
        high, low = halves(weight_of[i])
        parts = digits(
            (place // 65536, place // 256 % 256, place % 256, slot // 256, slot % 256), hot
        ) + [hot * high, hot * low]
        found = found + across(one_hot(order // LANES, places), jnp.concatenate(parts, axis=0))
        parts = digits((node_now // LANES, node_now % LANES), one_hot(slot % LANES, LANES))
        nodes = nodes + across(one_hot(slot // LANES, slots), jnp.concatenate(parts, axis=0))
        return base, found, nodes

    base = jnp.concatenate([jnp.zeros((devices, 1), f32), starts], axis=0)
    _, found, nodes = lax.fori_loop(
        0,
        chunks,
        chunk,
        (base, jnp.zeros((places, 7 * LANES), f32), jnp.zeros((slots, 2 * LANES), f32)),
        unroll=UNROLL,
    )
    part = [found[:, k * LANES : (k + 1) * LANES] for k in range(7)]
    place = (part[0] * 65536.0 + part[1] * 256.0 + part[2]).astype(jnp.int32)
    values = (
        place // cols,
        place % cols,
        (part[3] * 256.0 + part[4]).astype(jnp.int32),
        part[5] + part[6],
    )
    per = SPAN // LANES
    for to, value in zip(sorted_to, values):
        for i in range(spans):
            to[i] = jnp.concatenate([value[i * per + k : i * per + k + 1] for k in range(per)], axis=1)

    band_of = iota((SUB, LANES), 0)
    last = jnp.maximum((ends.astype(jnp.int32) + SPAN - 1) // SPAN - 1, 0)
    down = (last + band_of < iota((SUB, LANES), 1)) & (band_of < BANDS - 1)
    bands = jnp.sum(jnp.where(down, 1.0, 0.0), axis=0, keepdims=True).astype(jnp.int32)
    spans_of = jnp.minimum(iota((1, LANES), 1) - bands, spans - 1)
    meeting[...] = jnp.where(band_of == 0, spans_of, bands)
    return nodes[:, :LANES] * float(LANES) + nodes[:, LANES:]


def step_kernel(
    cell_in, dest_in, node_in, weight_in, depth_in, cond_in, wet_in, operator_in,
    target, adj, land_out, ocean_out,
    cell, dest, node, weight_of, cell_row, cell_col, slot, weight, meeting, table,
    land, cond, wet, held,
    ext, masked, found, col_hot, slot_row, slot_lane, packs, got, node_row, node_lane,
    out_edge, in_edge, cur, terms, hot, summed, parts,
    loads, edge_sends, edge_recvs, pack_sends, pack_recvs, sends, recvs,
):
    group, sea = lax.axis_size("sea"), lax.axis_index("sea")
    lands, row_of = lax.axis_size("land"), lax.axis_index("land")
    devices, me = group * lands, row_of * group + sea
    rows, cols = land.shape
    blocks, width = adj.shape
    kb = held.shape[1]
    planes, capr = got.shape[0], got.shape[2]
    spans, got_chunks = cell_row.shape[0], node_row.shape[0]
    bands, band = masked.shape[0], masked.shape[1]
    lines = COUNT // LANES
    west, east = beside_of("sea")
    north, south = beside_of("land")

    pairs = [
        (cell_in, cell), (dest_in, dest), (node_in, node), (weight_in, weight_of),
        (operator_in, held), (depth_in, land), (wet_in.at[0], wet.at[0]), (cond_in, cond),
    ] + [(wet_in.at[t], wet.at[t]) for t in range(1, STEPS)]
    load = [pltpu.make_async_copy(a, b, loads.at[i]) for i, (a, b) in enumerate(pairs)]
    for copy in load:
        copy.start()

    barrier = pltpu.get_barrier_semaphore()

    def greet(d, _):
        to = partner_of(lax.rem(me + d, devices))
        pl.semaphore_signal(barrier, inc=1, device_id=to, device_id_type=MESH)
        return 0

    lax.fori_loop(1, devices, greet, 0, unroll=True)

    cur[...] = adj[...]
    for s in range(group):
        hot[s * blocks : (s + 1) * blocks, :] = one_hot(target[...] - s * blocks, blocks)
    steps_to = sorted(range(1, group), key=lambda d: abs(2 * d - group))
    others = [lax.rem(sea + d, group) for d in steps_to]

    def shares(t):
        return [
            pltpu.make_async_remote_copy(
                src_ref=summed.at[t, to],
                dst_ref=parts.at[t, i],
                send_sem=sends.at[t, i],
                recv_sem=recvs.at[t, i],
                device_id={"sea": to},
                device_id_type=MESH,
            )
            for i, to in enumerate(others)
        ]

    def step_terms(t):
        tall = 16
        sub = iota((tall, width), 0)
        for g in range(blocks // tall):
            own = cur[g * tall : (g + 1) * tall, :]
            wide = jnp.concatenate(
                [jnp.where(sub == j, own, 0.0).astype(bf16) for j in range(tall)], axis=1
            )
            for k in range(kb):
                block = held[g * tall : (g + 1) * tall, k].reshape(tall * width, width)
                terms[k * blocks + g * tall : k * blocks + (g + 1) * tall, :] = jnp.dot(
                    wide, block, preferred_element_type=f32
                )
        both = jnp.concatenate(halves(terms[...]), axis=1)
        total = jnp.dot(hot[...], both, preferred_element_type=f32)
        for s in range(group):
            part = total[s * blocks : (s + 1) * blocks]
            summed[t, s] = part[:, :width] + part[:, width:]
        for copy in shares(t):
            copy.start()

    def send_plane(p, slots):
        for d in range(packs.shape[1]):
            packs[p, d] = slots[d * capr : (d + 1) * capr]

        def send(d, _):
            index = lax.rem(me + d, devices)
            pltpu.make_async_remote_copy(
                src_ref=packs.at[p, index],
                dst_ref=got.at[p, me],
                send_sem=pack_sends.at[p],
                recv_sem=pack_recvs.at[p],
                device_id=partner_of(index),
                device_id_type=MESH,
            ).start()
            return 0

        lax.fori_loop(1, devices, send, 0, unroll=True)
        got[p, me] = packs[p, me]

    def arrived(p):
        pltpu.make_async_remote_copy(
            src_ref=packs.at[p, pl.ds(0, devices - 1)],
            dst_ref=got.at[p, pl.ds(0, devices - 1)],
            send_sem=pack_sends.at[p],
            recv_sem=pack_recvs.at[p],
            device_id=partner_of(lax.rem(me + 1, devices)),
            device_id_type=MESH,
        ).wait()

    def line(p, i):
        return jnp.concatenate(
            [got[p, i * lines // capr + k // capr, pl.ds(k % capr, 1), :] for k in range(lines)],
            axis=1,
        )

    def edges(t):
        return [
            pltpu.make_async_remote_copy(
                src_ref=out_edge.at[t, i],
                dst_ref=in_edge.at[t, i ^ 1],
                send_sem=edge_sends.at[t, i],
                recv_sem=edge_recvs.at[t, i ^ 1],
                device_id=to,
                device_id_type=MESH,
            )
            for i, to in enumerate(
                ({"land": north}, {"land": south}, {"sea": west}, {"sea": east})
            )
        ]

    def spread_of(t):
        masked_step = wet[t].astype(f32) * land[...]
        for b in range(bands):
            masked[b] = masked_step[b * band : (b + 1) * band].astype(bf16)
        ext[SUB : SUB + rows, LANES : LANES + cols] = cond[...] * masked_step
        first = ext[SUB : SUB + rows, LANES : 2 * LANES]
        last = ext[SUB : SUB + rows, cols : cols + LANES]
        sides = jnp.where(iota((rows, LANES), 1) < LANES // 2, first, last).T
        out_edge[t, 0] = ext[SUB : SUB + 1, LANES : LANES + cols]
        out_edge[t, 1] = ext[SUB + rows - 1 : SUB + rows, LANES : LANES + cols]
        out_edge[t, 2] = sides[0:1]
        out_edge[t, 3] = sides[LANES - 1 :]
        for copy in edges(t):
            copy.start()

    def land_step(t):
        for copy in edges(t):
            copy.wait()
        has = [jnp.where(c, 1.0, 0.0) for c in (row_of > 0, row_of < lands - 1, sea > 0, sea < group - 1)]
        ext[SUB - 1 : SUB, LANES : LANES + cols] = in_edge[t, 0] * has[0]
        ext[SUB + rows : SUB + rows + 1, LANES : LANES + cols] = in_edge[t, 1] * has[1]
        sub = iota((LANES, rows), 0)
        sides = jnp.where(
            sub == LANES - 1,
            in_edge[t, 2] * has[2],
            jnp.where(sub == 0, in_edge[t, 3] * has[3], 0.0),
        ).T
        ext[SUB : SUB + rows, 0:LANES] = sides
        ext[SUB : SUB + rows, LANES + cols :] = sides
        tall = min(rows, 128)
        for r in range(0, rows, tall):
            a = SUB + r
            spread = ext[a : a + tall, LANES : LANES + cols]
            beside = (
                ext[a - 1 : a - 1 + tall, LANES : LANES + cols]
                + ext[a + 1 : a + 1 + tall, LANES : LANES + cols]
                + ext[a : a + tall, LANES - 1 : LANES - 1 + cols]
                + ext[a : a + tall, LANES + 1 : LANES + 1 + cols]
            )
            land[r : r + tall] = land[r : r + tall] + (beside - 4.0 * spread)

    for copy in load[:4]:
        copy.wait()
    nodes = index_entries(
        cell, dest, node, weight_of, (cell_row, cell_col, slot, weight), meeting,
        capr, devices, rows, cols,
    )
    into_scalars = pltpu.make_async_copy(meeting, table, loads.at[0])
    into_scalars.start()
    pl.semaphore_wait(barrier, devices - 1)
    send_plane(planes - 1, nodes)

    def index_span(i, _):
        col_hot[i] = one_hot(cell_col[i], cols)
        slot_row[i] = one_hot(slot[i] // LANES, slot_row.shape[1])
        slot_lane[i] = one_hot(slot[i] % LANES, LANES)
        return 0

    lax.fori_loop(0, spans, index_span, 0)
    into_scalars.wait()

    def flux_plane(t):
        def pair(p, _):
            i = jnp.clip(table[0, p], 0, spans - 1)
            b = jnp.clip(table[1, p], 0, bands - 1)
            lines = jnp.dot(masked[b], col_hot[i], preferred_element_type=f32)
            here = iota((band, SPAN), 0) == cell_row[i] - b * band
            line = jnp.sum(jnp.where(here, lines, 0.0), axis=0, keepdims=True)
            found[...] += jnp.where(iota((spans, SPAN), 0) == i, line, 0.0)
            return 0

        found[...] = jnp.zeros_like(found)
        lax.fori_loop(0, spans + bands - 1, pair, 0, unroll=True)
        slots = jnp.zeros((slot_row.shape[1], LANES), f32)
        for i in range(spans):
            flux = (weight[i] * found[i : i + 1, :]).astype(bf16)
            slots = slots + across(slot_row[i], slot_lane[i] * flux)
        send_plane(t, slots)

    def node_hots():
        arrived(planes - 1)

        def chunk(i, _):
            place = line(planes - 1, i).astype(jnp.int32)
            node_row[i] = one_hot(place // LANES, blocks)
            node_lane[i] = one_hot(place % LANES, LANES)
            return 0

        lax.fori_loop(0, got_chunks, chunk, 0)

    def ocean_step(t):
        arrived(t)

        def chunk(i, acc):
            return acc + across(node_row[i], node_lane[i] * line(t, i).astype(bf16))

        coupled = lax.fori_loop(0, got_chunks, chunk, jnp.zeros((blocks, width), f32), unroll=True)
        result = 0.5 * cur[...] + coupled + summed[t, sea]
        for copy in shares(t):
            copy.wait()
        for i in range(group - 1):
            result = result + parts[t, i]
        cur[...] = result

    for copy in load[4:]:
        copy.wait()
    store = pltpu.make_async_copy(land, land_out, loads.at[0])

    def step(t, _):
        before, ahead = t > 0, t < STEPS

        @pl.when(before)
        def _():
            land_step(t - 1)

        @pl.when(ahead)
        def _():
            spread_of(t)
            flux_plane(t)

        @pl.when(t == STEPS)
        def _():
            store.start()

        @pl.when(before)
        def _():
            ocean_step(t - 1)

        @pl.when(ahead)
        def _():
            step_terms(t)

        @pl.when(t == 0)
        def _():
            node_hots()

        return 0

    lax.fori_loop(0, STEPS + 1, step, 0)
    ocean_out[...] = cur[...]
    store.wait()


def finish_kernel(land, ocean, land_out, ocean_out, held, kept, sems):
    rows, tall = land.shape[0], land.shape[0] // 4
    moves = [(land.at[pl.ds(r, tall)], held.at[pl.ds(r, tall)], land_out.at[pl.ds(r, tall)]) for r in range(0, rows, tall)]
    moves.append((ocean, kept, ocean_out))
    into = [pltpu.make_async_copy(a, b, sems.at[0, i]) for i, (a, b, _) in enumerate(moves)]
    out = [pltpu.make_async_copy(b, c, sems.at[1, i]) for i, (_, b, c) in enumerate(moves)]
    for copy in into:
        copy.start()
    for first, second in zip(into, out):
        first.wait()
        second.start()
    for copy in out:
        copy.wait()


def finish(land, ocean):
    anywhere = pl.BlockSpec(memory_space=pl.ANY)
    return tuple(
        pl.pallas_call(
            finish_kernel,
            out_shape=(
                jax.ShapeDtypeStruct(land.shape, f32),
                jax.ShapeDtypeStruct(ocean.shape, f32),
            ),
            in_specs=[anywhere] * 2,
            out_specs=(anywhere, anywhere),
            scratch_shapes=[
                pltpu.VMEM(land.shape, f32),
                pltpu.VMEM(ocean.shape, f32),
                pltpu.SemaphoreType.DMA((2, 5)),
            ],
            name="results",
        )(land, ocean)
    )


def local(
    adj_depth,
    conductance,
    wet,
    coast_cell,
    coast_dest,
    coast_node,
    coast_weight,
    adj_ocean,
    ocean_blocks,
    ocean_target,
):
    group, devices = lax.axis_size("sea"), lax.axis_size(("land", "sea"))
    rows, cols = adj_depth.shape
    blocks, width = adj_ocean.shape
    kb = ocean_blocks.shape[1]
    entries = coast_cell.shape[0]
    capr = 2 * entries // devices // LANES
    slots = devices * capr
    planes = STEPS + 1
    line, span = (entries // COUNT, 1, COUNT), (entries // SPAN, 1, SPAN)
    spans = span[0]
    vmem, anywhere = pl.BlockSpec(memory_space=pltpu.VMEM), pl.BlockSpec(memory_space=pl.ANY)
    land, ocean = pl.pallas_call(
        step_kernel,
        out_shape=(
            jax.ShapeDtypeStruct((rows, cols), f32),
            jax.ShapeDtypeStruct((blocks, width), f32),
        ),
        in_specs=[anywhere] * 8 + [vmem] * 2,
        out_specs=(anywhere, vmem),
        scratch_shapes=[
            pltpu.VMEM(line, jnp.int32),
            pltpu.VMEM(line, jnp.int32),
            pltpu.VMEM(line, jnp.int32),
            pltpu.VMEM(line, f32),
            pltpu.VMEM(span, jnp.int32),
            pltpu.VMEM(span, jnp.int32),
            pltpu.VMEM(span, jnp.int32),
            pltpu.VMEM(span, f32),
            pltpu.VMEM((SUB, LANES), jnp.int32),
            pltpu.SMEM((SUB, LANES), jnp.int32),
            pltpu.VMEM((rows, cols), f32),
            pltpu.VMEM((rows, cols), f32),
            pltpu.VMEM((STEPS, rows, cols), jnp.int32),
            pltpu.VMEM(ocean_blocks.shape, bf16),
            pltpu.VMEM((rows + 2 * SUB, cols + 2 * LANES), f32),
            pltpu.VMEM((BANDS, rows // BANDS, cols), bf16),
            pltpu.VMEM((spans, SPAN), f32),
            pltpu.VMEM((spans, cols, SPAN), bf16),
            pltpu.VMEM((spans, slots, SPAN), bf16),
            pltpu.VMEM((spans, LANES, SPAN), bf16),
            pltpu.VMEM((planes, devices, capr, LANES), f32),
            pltpu.VMEM((planes, devices, capr, LANES), f32),
            pltpu.VMEM((slots * LANES // COUNT, blocks, COUNT), bf16),
            pltpu.VMEM((slots * LANES // COUNT, LANES, COUNT), bf16),
            pltpu.VMEM((STEPS, 4, 1, max(rows, cols)), f32),
            pltpu.VMEM((STEPS, 4, 1, max(rows, cols)), f32),
            pltpu.VMEM((blocks, width), f32),
            pltpu.VMEM((kb * blocks, width), f32),
            pltpu.VMEM((group * blocks, kb * blocks), bf16),
            pltpu.VMEM((STEPS, group, blocks, width), f32),
            pltpu.VMEM((STEPS, group - 1, blocks, width), f32),
            pltpu.SemaphoreType.DMA((8 + STEPS - 1,)),
            pltpu.SemaphoreType.DMA((STEPS, 4)),
            pltpu.SemaphoreType.DMA((STEPS, 4)),
            pltpu.SemaphoreType.DMA((planes,)),
            pltpu.SemaphoreType.DMA((planes,)),
            pltpu.SemaphoreType.DMA((STEPS, group - 1)),
            pltpu.SemaphoreType.DMA((STEPS, group - 1)),
        ],
        compiler_params=pltpu.CompilerParams(
            vmem_limit_bytes=58 << 20, collective_id=0, has_side_effects=True
        ),
        name="adjoint_steps",
    )(
        coast_cell.reshape(line),
        coast_dest.reshape(line),
        coast_node.reshape(line),
        coast_weight.reshape(line),
        adj_depth,
        conductance,
        wet,
        ocean_blocks,
        ocean_target.T.reshape(1, -1),
        adj_ocean,
    )
    return finish(land, ocean)


def solution(mesh):
    in_specs = (
        P("land", "sea"),
        P("land", "sea"),
        P(None, "land", "sea"),
        P(("land", "sea")),
        P(("land", "sea"), None),
        P(("land", "sea")),
        P(("land", "sea")),
        P(("land", "sea"), None),
        P(("land", "sea"), None, None, None),
        P(("land", "sea"), None),
    )
    out_specs = (P("land", "sea"), P(("land", "sea"), None))
    return jax.shard_map(local, mesh=mesh, in_specs=in_specs, out_specs=out_specs, check_vma=False)
```

```python
import jax
import jax.numpy as jnp
from jax import lax
from jax.experimental import pallas as pl
from jax.experimental.pallas import tpu as pltpu
from jax.sharding import PartitionSpec as P

STEPS = 4
LANES = 128
SUB = 8
COUNT = 1024
PIECE = 256
SPAN = 512
BANDS = 4
UNROLL = True
MESH = pl.DeviceIdType.MESH
f32, bf16 = jnp.float32, jnp.bfloat16


def iota(shape, axis):
    return lax.broadcasted_iota(jnp.int32, shape, axis)


def halves(value):
    high = value.astype(bf16)
    return high, (value - high.astype(f32)).astype(bf16)


def across(a, b):
    return lax.dot_general(a, b, (((1,), (1,)), ((), ())), preferred_element_type=f32)


def one_hot(index, size):
    parts = []
    for first in range(0, size, 256):
        at = iota((min(256, size - first), index.shape[1]), 0).astype(f32).astype(bf16)
        here = at == (index - first).astype(f32).astype(bf16)
        parts.append(jnp.where(here, jnp.ones((), bf16), jnp.zeros((), bf16)))
    return parts[0] if len(parts) == 1 else jnp.concatenate(parts, axis=0)


def beside_of(axis):
    count, me = lax.axis_size(axis), lax.axis_index(axis)
    return lax.rem(me + count - 1, count), lax.rem(me + 1, count)


def partner_of(index):
    seas = lax.axis_size("sea")
    return {"land": index // seas, "sea": lax.rem(index, seas)}


def index_entries(cell, dest, node, weight_of, sorted_to, meeting, capr, devices, rows, cols):
    chunks = cell.shape[0]
    spans, places = chunks * COUNT // SPAN, chunks * COUNT // LANES
    capacity, slots = capr * LANES, devices * capr
    band = rows // BANDS * cols
    sub = iota((SUB, COUNT), 0)

    ends = starts = jnp.zeros((SUB, COUNT), f32)
    for i in range(chunks):
        at = cell[i] // band
        ends = ends + jnp.where(at <= sub, 1.0, 0.0)
        starts = starts + jnp.where(at < sub, 1.0, 0.0)
    ends = jnp.sum(ends, axis=1, keepdims=True)
    starts = jnp.sum(starts, axis=1, keepdims=True)

    triangle = jnp.where(iota((PIECE, PIECE), 0) <= iota((PIECE, PIECE), 1), 1.0, 0.0).astype(bf16)

    def digits(values, hot):
        return [hot * v.astype(f32).astype(bf16) for v in values]

    def chunk(i, carry):
        base, found, nodes = carry
        dest_now, place, node_now = dest[i], cell[i], node[i]
        matches = jnp.concatenate(
            [
                jnp.where(iota((devices, COUNT), 0) == dest_now, 1.0, 0.0),
                jnp.where(sub == place // band, 1.0, 0.0),
            ],
            axis=0,
        )
        ranks, orders = [], []
        for p in range(0, COUNT, PIECE):
            own = matches[:, p : p + PIECE]
            running = jnp.dot(own.astype(bf16), triangle, preferred_element_type=f32)
            counted = own * (running + base)
            ranks.append(jnp.sum(counted[:devices], axis=0, keepdims=True))
            orders.append(jnp.sum(counted[devices:], axis=0, keepdims=True))
            base = base + jnp.sum(own, axis=1, keepdims=True)
        slot = dest_now * capacity + jnp.concatenate(ranks, axis=1).astype(jnp.int32) - 1
        order = jnp.concatenate(orders, axis=1).astype(jnp.int32) - 1
        hot = one_hot(order % LANES, LANES)
        high, low = halves(weight_of[i])
        parts = digits(
            (place // 65536 * 64 + slot // 256, place // 256 % 256, place % 256, slot % 256), hot
        ) + [hot * high, hot * low]
        found = found + across(one_hot(order // LANES, places), jnp.concatenate(parts, axis=0))
        parts = digits((node_now // LANES, node_now % LANES), one_hot(slot % LANES, LANES))
        nodes = nodes + across(one_hot(slot // LANES, slots), jnp.concatenate(parts, axis=0))
        return base, found, nodes

    base = jnp.concatenate([jnp.zeros((devices, 1), f32), starts], axis=0)
    _, found, nodes = lax.fori_loop(
        0,
        chunks,
        chunk,
        (base, jnp.zeros((places, 6 * LANES), f32), jnp.zeros((slots, 2 * LANES), f32)),
        unroll=UNROLL,
    )
    part = [found[:, k * LANES : (k + 1) * LANES] for k in range(6)]
    top = part[0].astype(jnp.int32)
    place = top // 64 * 65536 + (part[1] * 256.0 + part[2]).astype(jnp.int32)
    values = (
        place // cols,
        place % cols,
        top % 64 * 256 + part[3].astype(jnp.int32),
        part[4] + part[5],
    )
    per = SPAN // LANES
    for to, value in zip(sorted_to, values):
        for i in range(spans):
            to[i] = jnp.concatenate([value[i * per + k : i * per + k + 1] for k in range(per)], axis=1)

    band_of = iota((SUB, LANES), 0)
    last = jnp.maximum((ends.astype(jnp.int32) + SPAN - 1) // SPAN - 1, 0)
    down = (last + band_of < iota((SUB, LANES), 1)) & (band_of < BANDS - 1)
    bands = jnp.sum(jnp.where(down, 1.0, 0.0), axis=0, keepdims=True).astype(jnp.int32)
    spans_of = jnp.minimum(iota((1, LANES), 1) - bands, spans - 1)
    meeting[...] = jnp.where(band_of == 0, spans_of, bands)
    return nodes[:, :LANES] * float(LANES) + nodes[:, LANES:]


def step_kernel(
    cell_in, dest_in, node_in, weight_in, depth_in, cond_in, wet_in, operator_in,
    target, adj, land_out, ocean_out,
    cell, dest, node, weight_of, cell_row, cell_col, slot, weight, meeting, table,
    land, cond, wet, held,
    ext, masked, col_hot, slot_row, slot_lane, packs, got, node_row, node_lane,
    out_edge, in_edge, cur, terms, hot, summed, parts,
    loads, edge_sends, edge_recvs, pack_sends, pack_recvs, sends, recvs,
):
    group, sea = lax.axis_size("sea"), lax.axis_index("sea")
    lands, row_of = lax.axis_size("land"), lax.axis_index("land")
    devices, me = group * lands, row_of * group + sea
    rows, cols = land.shape
    blocks, width = adj.shape
    kb = held.shape[1]
    planes, capr = got.shape[0], got.shape[2]
    spans, got_chunks = cell_row.shape[0], node_row.shape[0]
    bands, band = masked.shape[0], masked.shape[1]
    lines = COUNT // LANES
    west, east = beside_of("sea")
    north, south = beside_of("land")

    pairs = [
        (cell_in, cell), (dest_in, dest), (node_in, node), (weight_in, weight_of),
        (operator_in, held), (depth_in, land), (wet_in.at[0], wet.at[0]), (cond_in, cond),
    ] + [(wet_in.at[t], wet.at[t]) for t in range(1, STEPS)]
    load = [pltpu.make_async_copy(a, b, loads.at[i]) for i, (a, b) in enumerate(pairs)]
    for copy in load:
        copy.start()

    barrier = pltpu.get_barrier_semaphore()

    def greet(d, _):
        to = partner_of(lax.rem(me + d, devices))
        pl.semaphore_signal(barrier, inc=1, device_id=to, device_id_type=MESH)
        return 0

    lax.fori_loop(1, devices, greet, 0, unroll=True)

    cur[...] = adj[...]
    for s in range(group):
        hot[s * blocks : (s + 1) * blocks, :] = one_hot(target[...] - s * blocks, blocks)
    steps_to = sorted(range(1, group), key=lambda d: abs(2 * d - group))
    others = [lax.rem(sea + d, group) for d in steps_to]

    def shares(t):
        return [
            pltpu.make_async_remote_copy(
                src_ref=summed.at[t, to],
                dst_ref=parts.at[t, i],
                send_sem=sends.at[t, i],
                recv_sem=recvs.at[t, i],
                device_id={"sea": to},
                device_id_type=MESH,
            )
            for i, to in enumerate(others)
        ]

    def step_terms(t):
        tall = 16
        sub = iota((tall, width), 0)
        for g in range(blocks // tall):
            own = cur[g * tall : (g + 1) * tall, :]
            wide = jnp.concatenate(
                [jnp.where(sub == j, own, 0.0).astype(bf16) for j in range(tall)], axis=1
            )
            for k in range(kb):
                block = held[g * tall : (g + 1) * tall, k].reshape(tall * width, width)
                terms[k * blocks + g * tall : k * blocks + (g + 1) * tall, :] = jnp.dot(
                    wide, block, preferred_element_type=f32
                )
        both = jnp.concatenate(halves(terms[...]), axis=1)
        total = jnp.dot(hot[...], both, preferred_element_type=f32)
        for s in range(group):
            part = total[s * blocks : (s + 1) * blocks]
            summed[t, s] = part[:, :width] + part[:, width:]
        for copy in shares(t):
            copy.start()

    def send_plane(p, slots):
        for d in range(packs.shape[1]):
            packs[p, d] = slots[d * capr : (d + 1) * capr]

        def send(d, _):
            index = lax.rem(me + d, devices)
            pltpu.make_async_remote_copy(
                src_ref=packs.at[p, index],
                dst_ref=got.at[p, me],
                send_sem=pack_sends.at[p],
                recv_sem=pack_recvs.at[p],
                device_id=partner_of(index),
                device_id_type=MESH,
            ).start()
            return 0

        lax.fori_loop(1, devices, send, 0, unroll=True)
        got[p, me] = packs[p, me]

    def arrived(p):
        pltpu.make_async_remote_copy(
            src_ref=packs.at[p, pl.ds(0, devices - 1)],
            dst_ref=got.at[p, pl.ds(0, devices - 1)],
            send_sem=pack_sends.at[p],
            recv_sem=pack_recvs.at[p],
            device_id=partner_of(lax.rem(me + 1, devices)),
            device_id_type=MESH,
        ).wait()

    def line(p, i):
        return jnp.concatenate(
            [got[p, i * lines // capr + k // capr, pl.ds(k % capr, 1), :] for k in range(lines)],
            axis=1,
        )

    def edges(t):
        return [
            pltpu.make_async_remote_copy(
                src_ref=out_edge.at[t, i],
                dst_ref=in_edge.at[t, i ^ 1],
                send_sem=edge_sends.at[t, i],
                recv_sem=edge_recvs.at[t, i ^ 1],
                device_id=to,
                device_id_type=MESH,
            )
            for i, to in enumerate(
                ({"land": north}, {"land": south}, {"sea": west}, {"sea": east})
            )
        ]

    def spread_of(t):
        masked_step = wet[t].astype(f32) * land[...]
        for b in range(bands):
            masked[b] = masked_step[b * band : (b + 1) * band].astype(bf16)
        ext[SUB : SUB + rows, LANES : LANES + cols] = cond[...] * masked_step
        first = ext[SUB : SUB + rows, LANES : 2 * LANES]
        last = ext[SUB : SUB + rows, cols : cols + LANES]
        sides = jnp.where(iota((rows, LANES), 1) < LANES // 2, first, last).T
        out_edge[t, 0] = ext[SUB : SUB + 1, LANES : LANES + cols]
        out_edge[t, 1] = ext[SUB + rows - 1 : SUB + rows, LANES : LANES + cols]
        out_edge[t, 2] = sides[0:1]
        out_edge[t, 3] = sides[LANES - 1 :]
        for copy in edges(t):
            copy.start()

    def land_step(t):
        for copy in edges(t):
            copy.wait()
        has = [jnp.where(c, 1.0, 0.0) for c in (row_of > 0, row_of < lands - 1, sea > 0, sea < group - 1)]
        ext[SUB - 1 : SUB, LANES : LANES + cols] = in_edge[t, 0] * has[0]
        ext[SUB + rows : SUB + rows + 1, LANES : LANES + cols] = in_edge[t, 1] * has[1]
        sub = iota((LANES, rows), 0)
        sides = jnp.where(
            sub == LANES - 1,
            in_edge[t, 2] * has[2],
            jnp.where(sub == 0, in_edge[t, 3] * has[3], 0.0),
        ).T
        ext[SUB : SUB + rows, 0:LANES] = sides
        ext[SUB : SUB + rows, LANES + cols :] = sides
        tall = min(rows, 128)
        for r in range(0, rows, tall):
            a = SUB + r
            spread = ext[a : a + tall, LANES : LANES + cols]
            beside = (
                ext[a - 1 : a - 1 + tall, LANES : LANES + cols]
                + ext[a + 1 : a + 1 + tall, LANES : LANES + cols]
                + ext[a : a + tall, LANES - 1 : LANES - 1 + cols]
                + ext[a : a + tall, LANES + 1 : LANES + 1 + cols]
            )
            land[r : r + tall] = land[r : r + tall] + (beside - 4.0 * spread)

    for copy in load[:4]:
        copy.wait()
    nodes = index_entries(
        cell, dest, node, weight_of, (cell_row, cell_col, slot, weight), meeting,
        capr, devices, rows, cols,
    )
    into_scalars = pltpu.make_async_copy(meeting, table, loads.at[0])
    into_scalars.start()
    pl.semaphore_wait(barrier, devices - 1)
    send_plane(planes - 1, nodes)

    def index_span(i, _):
        col_hot[i] = one_hot(cell_col[i], cols)
        slot_row[i] = one_hot(slot[i] // LANES, slot_row.shape[1])
        slot_lane[i] = one_hot(slot[i] % LANES, LANES)
        return 0

    lax.fori_loop(0, spans, index_span, 0)
    into_scalars.wait()

    def flux_plane(t):
        def pair(p, total):
            i = jnp.clip(table[0, p], 0, spans - 1)
            b = jnp.clip(table[1, p], 0, bands - 1)
            lines = jnp.dot(masked[b], col_hot[i], preferred_element_type=f32)
            here = iota((band, SPAN), 0) == cell_row[i] - b * band
            line = jnp.sum(jnp.where(here, lines, 0.0), axis=0, keepdims=True)
            return total + jnp.where(iota((spans, SPAN), 0) == i, line, 0.0)

        found = lax.fori_loop(
            0, spans + bands - 1, pair, jnp.zeros((spans, SPAN), f32), unroll=True
        )
        slots = jnp.zeros((slot_row.shape[1], LANES), f32)
        for i in range(spans):
            flux = (weight[i] * found[i : i + 1, :]).astype(bf16)
            slots = slots + across(slot_row[i], slot_lane[i] * flux)
        send_plane(t, slots)

    def node_hots():
        arrived(planes - 1)

        def chunk(i, _):
            place = line(planes - 1, i).astype(jnp.int32)
            node_row[i] = one_hot(place // LANES, blocks)
            node_lane[i] = one_hot(place % LANES, LANES)
            return 0

        lax.fori_loop(0, got_chunks, chunk, 0)

    def ocean_step(t):
        arrived(t)

        def chunk(i, acc):
            return acc + across(node_row[i], node_lane[i] * line(t, i).astype(bf16))

        coupled = lax.fori_loop(0, got_chunks, chunk, jnp.zeros((blocks, width), f32), unroll=True)
        result = 0.5 * cur[...] + coupled + summed[t, sea]
        for copy in shares(t):
            copy.wait()
        for i in range(group - 1):
            result = result + parts[t, i]
        cur[...] = result

    for copy in load[4:]:
        copy.wait()
    store = pltpu.make_async_copy(land, land_out, loads.at[0])

    def step(t, _):
        before, ahead = t > 0, t < STEPS

        @pl.when(before)
        def _():
            land_step(t - 1)

        @pl.when(ahead)
        def _():
            spread_of(t)
            flux_plane(t)

        @pl.when(t == STEPS)
        def _():
            store.start()

        @pl.when(before)
        def _():
            ocean_step(t - 1)

        @pl.when(ahead)
        def _():
            step_terms(t)

        @pl.when(t == 0)
        def _():
            node_hots()

        return 0

    lax.fori_loop(0, STEPS + 1, step, 0)
    ocean_out[...] = cur[...]
    store.wait()


def finish_kernel(land, ocean, land_out, ocean_out, held, kept, sems):
    rows, tall = land.shape[0], land.shape[0] // 4
    moves = [(land.at[pl.ds(r, tall)], held.at[pl.ds(r, tall)], land_out.at[pl.ds(r, tall)]) for r in range(0, rows, tall)]
    moves.append((ocean, kept, ocean_out))
    into = [pltpu.make_async_copy(a, b, sems.at[0, i]) for i, (a, b, _) in enumerate(moves)]
    out = [pltpu.make_async_copy(b, c, sems.at[1, i]) for i, (_, b, c) in enumerate(moves)]
    for copy in into:
        copy.start()
    for first, second in zip(into, out):
        first.wait()
        second.start()
    for copy in out:
        copy.wait()


def finish(land, ocean):
    anywhere = pl.BlockSpec(memory_space=pl.ANY)
    return tuple(
        pl.pallas_call(
            finish_kernel,
            out_shape=(
                jax.ShapeDtypeStruct(land.shape, f32),
                jax.ShapeDtypeStruct(ocean.shape, f32),
            ),
            in_specs=[anywhere] * 2,
            out_specs=(anywhere, anywhere),
            scratch_shapes=[
                pltpu.VMEM(land.shape, f32),
                pltpu.VMEM(ocean.shape, f32),
                pltpu.SemaphoreType.DMA((2, 5)),
            ],
            name="results",
        )(land, ocean)
    )


def local(
    adj_depth,
    conductance,
    wet,
    coast_cell,
    coast_dest,
    coast_node,
    coast_weight,
    adj_ocean,
    ocean_blocks,
    ocean_target,
):
    group, devices = lax.axis_size("sea"), lax.axis_size(("land", "sea"))
    rows, cols = adj_depth.shape
    blocks, width = adj_ocean.shape
    kb = ocean_blocks.shape[1]
    entries = coast_cell.shape[0]
    capr = 2 * entries // devices // LANES
    slots = devices * capr
    planes = STEPS + 1
    line, span = (entries // COUNT, 1, COUNT), (entries // SPAN, 1, SPAN)
    spans = span[0]
    vmem, anywhere = pl.BlockSpec(memory_space=pltpu.VMEM), pl.BlockSpec(memory_space=pl.ANY)
    land, ocean = pl.pallas_call(
        step_kernel,
        out_shape=(
            jax.ShapeDtypeStruct((rows, cols), f32),
            jax.ShapeDtypeStruct((blocks, width), f32),
        ),
        in_specs=[anywhere] * 8 + [vmem] * 2,
        out_specs=(anywhere, vmem),
        scratch_shapes=[
            pltpu.VMEM(line, jnp.int32),
            pltpu.VMEM(line, jnp.int32),
            pltpu.VMEM(line, jnp.int32),
            pltpu.VMEM(line, f32),
            pltpu.VMEM(span, jnp.int32),
            pltpu.VMEM(span, jnp.int32),
            pltpu.VMEM(span, jnp.int32),
            pltpu.VMEM(span, f32),
            pltpu.VMEM((SUB, LANES), jnp.int32),
            pltpu.SMEM((SUB, LANES), jnp.int32),
            pltpu.VMEM((rows, cols), f32),
            pltpu.VMEM((rows, cols), f32),
            pltpu.VMEM((STEPS, rows, cols), jnp.int32),
            pltpu.VMEM(ocean_blocks.shape, bf16),
            pltpu.VMEM((rows + 2 * SUB, cols + 2 * LANES), f32),
            pltpu.VMEM((BANDS, rows // BANDS, cols), bf16),
            pltpu.VMEM((spans, cols, SPAN), bf16),
            pltpu.VMEM((spans, slots, SPAN), bf16),
            pltpu.VMEM((spans, LANES, SPAN), bf16),
            pltpu.VMEM((planes, devices, capr, LANES), f32),
            pltpu.VMEM((planes, devices, capr, LANES), f32),
            pltpu.VMEM((slots * LANES // COUNT, blocks, COUNT), bf16),
            pltpu.VMEM((slots * LANES // COUNT, LANES, COUNT), bf16),
            pltpu.VMEM((STEPS, 4, 1, max(rows, cols)), f32),
            pltpu.VMEM((STEPS, 4, 1, max(rows, cols)), f32),
            pltpu.VMEM((blocks, width), f32),
            pltpu.VMEM((kb * blocks, width), f32),
            pltpu.VMEM((group * blocks, kb * blocks), bf16),
            pltpu.VMEM((STEPS, group, blocks, width), f32),
            pltpu.VMEM((STEPS, group - 1, blocks, width), f32),
            pltpu.SemaphoreType.DMA((8 + STEPS - 1,)),
            pltpu.SemaphoreType.DMA((STEPS, 4)),
            pltpu.SemaphoreType.DMA((STEPS, 4)),
            pltpu.SemaphoreType.DMA((planes,)),
            pltpu.SemaphoreType.DMA((planes,)),
            pltpu.SemaphoreType.DMA((STEPS, group - 1)),
            pltpu.SemaphoreType.DMA((STEPS, group - 1)),
        ],
        compiler_params=pltpu.CompilerParams(
            vmem_limit_bytes=58 << 20, collective_id=0, has_side_effects=True
        ),
        name="adjoint_steps",
    )(
        coast_cell.reshape(line),
        coast_dest.reshape(line),
        coast_node.reshape(line),
        coast_weight.reshape(line),
        adj_depth,
        conductance,
        wet,
        ocean_blocks,
        ocean_target.T.reshape(1, -1),
        adj_ocean,
    )
    return finish(land, ocean)


def solution(mesh):
    in_specs = (
        P("land", "sea"),
        P("land", "sea"),
        P(None, "land", "sea"),
        P(("land", "sea")),
        P(("land", "sea"), None),
        P(("land", "sea")),
        P(("land", "sea")),
        P(("land", "sea"), None),
        P(("land", "sea"), None, None, None),
        P(("land", "sea"), None),
    )
    out_specs = (P("land", "sea"), P(("land", "sea"), None))
    return jax.shard_map(local, mesh=mesh, in_specs=in_specs, out_specs=out_specs, check_vma=False)
```
